32 devices in a mesh: seq: 16 (over z, y, core), head: 2 (over x).
Axes of the slice: x: 2, y: 2, z: 4, core: 2. Of those that a mesh axis runs over, the one named last changes fastest.
Arguments:
- projected: bfloat16 [16384, 4096], P(('seq', 'head')), may hold values from -6 to 6
- conv_weight: bfloat16 [4, 4096], P(None, 'head'), may hold values from -3 to 3
- log_gate: float32 [16, 16384], P('head', 'seq'), may hold values from -0.9 to 0
- write_rate: float32 [16, 16384], P('head', 'seq'), may hold values from 0 to 0.9
- norm_gain: float32 [128], replicated, may hold values from 0.5 to 1.5
Outputs:
- mixed_out: bfloat16 [16384, 2048], P(('seq', 'head'))
The draws below stay inside these ranges and needn't reach their ends.
All inputs are finite; a program needn't handle non-finite values.
Results may differ from the reference program's by a relative error of at most 0.012.
Values may be sent and summed in bfloat16 or wider, within the bound.
No kernel may reach another device: no remote copies, remote signals or barrier semaphores. Data moves between devices by JAX's collectives and lax.ppermute only.
A program may use at most 64 MiB of HBM per device.

```python
import jax
import jax.numpy as jnp
from jax import lax

DK = 128
V_GROUP = 2
KW = 4
STRETCH = 128
L_DEV = 1024
VALUE_HEADS = 16
CH = 4096
TOKEN_COUNT = 16384


def slow_heads(key):
    branch = jax.random.fold_in(key, 7)
    return jax.random.randint(branch, (VALUE_HEADS, 1), 0, 2) > 0


def log_uniform(key, shape, low_end, high_end):
    return jnp.exp(jax.random.uniform(key, shape, jnp.float32, jnp.log(low_end), jnp.log(high_end)))


def draw_log_gate(key, part):
    slow = slow_heads(key)
    parallel_flows = jax.random.split(jax.random.fold_in(key, 11), 6)
    fast_rate = log_uniform(parallel_flows[0], (VALUE_HEADS, 1), 1.0 / 50.0, 1.0 / 30.0)
    slow_rate = log_uniform(parallel_flows[1], (VALUE_HEADS, 1), 0.05, 0.15) / TOKEN_COUNT
    head_rate = jnp.where(slow, slow_rate, fast_rate)
    device_factor = jnp.repeat(log_uniform(parallel_flows[2], (VALUE_HEADS, TOKEN_COUNT // L_DEV), 0.5, 2.0), L_DEV, axis=1)
    roughness = log_uniform(parallel_flows[3], (VALUE_HEADS, TOKEN_COUNT), 0.5, 2.0)
    gate_baseline = -head_rate * device_factor * roughness
    spike_pattern = jax.random.randint(parallel_flows[4], (VALUE_HEADS, TOKEN_COUNT), 0, TOKEN_COUNT) < 3
    discarded_entries = jnp.log(jax.random.uniform(parallel_flows[5], (VALUE_HEADS, TOKEN_COUNT), jnp.float32, 0.5, 0.8))
    return jnp.where(spike_pattern, gate_baseline + discarded_entries, gate_baseline)


def draw_write_rate(key, part):
    slow = slow_heads(key)
    parallel_flows = jax.random.split(jax.random.fold_in(key, 13), 4)
    fast_write = jax.random.uniform(parallel_flows[0], (VALUE_HEADS, TOKEN_COUNT), jnp.float32, 0.3, 0.9)
    total_share = log_uniform(parallel_flows[1], (VALUE_HEADS, 1), 2.0, 2.8) * DK / TOKEN_COUNT
    roughness = jax.random.uniform(parallel_flows[2], (VALUE_HEADS, TOKEN_COUNT), jnp.float32, 0.5, 1.5)
    active = jax.random.randint(parallel_flows[3], (VALUE_HEADS, TOKEN_COUNT), 0, 8) == 0
    slow_write = jnp.where(active, jnp.minimum(8.0 * total_share * roughness, 0.85), 0.0)
    return jnp.where(slow, slow_write, fast_write)


def levels(rng, extent, cuts, smallest, top_value):
    def one(dim, parts):
        steps = jax.random.uniform(jax.random.fold_in(jax.random.fold_in(rng, 6), dim), (parts,), jnp.float32, smallest / len(cuts), top_value / len(cuts))
        return jnp.repeat(jnp.exp(steps), extent[dim] // parts).reshape((-1,) + (1,) * (len(extent) - dim - 1))

    loudness = one(*cuts[0])
    for cut in cuts[1:]:
        loudness = loudness * one(*cut)
    return loudness


def gaussian(key, shape, scale, reach, shards=(), held_as=jnp.bfloat16):
    array = jax.random.normal(key, shape, jnp.float32) * scale
    if len(shards) > 0:
        array = levels(key, shape, shards, -0.22, 0.18) * array
    return jnp.clip(array, min=-reach, max=reach).astype(held_as)


def setup_inputs(seed: int = 0) -> dict:
    streams_of = jax.random.split(jax.random.key(seed), 6)
    projected = gaussian(streams_of[0], (TOKEN_COUNT, CH), 1.0, 6.0, ((0, 32),))
    conv_weight = gaussian(streams_of[1], (KW, CH), 0.5, 3.0, ((1, 2),))
    log_gate = draw_log_gate(jax.random.fold_in(streams_of[5], 71), 0)
    write_rate = draw_write_rate(jax.random.fold_in(streams_of[5], 71), 0)
    norm_gain = jnp.clip(1.0 + 0.1 * jax.random.normal(streams_of[4], (DK,), jnp.float32), 0.5, 1.5)
    return {"projected": projected, "conv_weight": conv_weight, "log_gate": log_gate, "write_rate": write_rate, "norm_gain": norm_gain}


PRECISE = lax.Precision.HIGHEST

def prepare(key_rows, values, gates, rates):
    span = key_rows.shape[-2]
    width = key_rows.shape[-1]
    cumulative = jnp.cumsum(gates, axis=-1)
    index_of_row = lax.broadcasted_iota(jnp.int32, (span, span), 0)
    col_index = lax.broadcasted_iota(jnp.int32, (span, span), 1)
    inside_mask = index_of_row >= col_index
    below_mask = index_of_row > col_index
    spread = cumulative[..., :, None] - cumulative[..., None, :]
    decay_mat = jnp.where(inside_mask, jnp.exp(jnp.where(inside_mask, spread, 0.0)), 0.0)
    intersection = jnp.einsum('...td,...sd->...ts', key_rows, key_rows, precision=PRECISE)
    lower_part = jnp.where(below_mask, rates[..., :, None] * intersection * decay_mat, 0.0)
    system = lower_part + jnp.eye(span, dtype=jnp.float32)
    right_side = jnp.concatenate([rates[..., None] * values, (rates * jnp.exp(cumulative))[..., None] * key_rows], axis=-1)
    solved = lax.linalg.triangular_solve(system, right_side, left_side=True, lower=True, unit_diagonal=True)
    return (cumulative, decay_mat, solved[..., :width], solved[..., width:])

def apply_state(queries, key_rows, cumulative, decay_mat, fresh, carried, state):
    written = fresh - jnp.einsum('...ce,...ef->...cf', carried, state, precision=PRECISE)
    scores = jnp.einsum('...td,...sd->...ts', queries, key_rows, precision=PRECISE) * decay_mat
    output = jnp.exp(cumulative)[..., None] * jnp.einsum('...cd,...de->...ce', queries, state, precision=PRECISE)
    output = output + jnp.einsum('...ts,...se->...te', scores, written, precision=PRECISE)
    return (output, written)

def head_rows(convolved):
    count_rows = convolved.shape[0]
    grouped = convolved.astype(jnp.float32).reshape(count_rows, -1, 2 + V_GROUP, DK)
    queries = grouped[:, :, 0]
    key_rows = grouped[:, :, 1]
    key_rows = key_rows * lax.rsqrt(lax.optimization_barrier(jnp.sum(key_rows * key_rows, axis=-1, keepdims=True)) + 1e-06)
    queries = jnp.repeat(queries, V_GROUP, axis=1)
    key_rows = jnp.repeat(key_rows, V_GROUP, axis=1)
    values = grouped[:, :, 2:].reshape(count_rows, -1, DK)
    return (jnp.transpose(queries, (1, 0, 2)), jnp.transpose(key_rows, (1, 0, 2)), jnp.transpose(values, (1, 0, 2)))

def normalize(output, norm_gain):
    return output * lax.rsqrt(lax.optimization_barrier(jnp.mean(output * output, axis=-1, keepdims=True)) + 1e-06) * norm_gain

def reference(projected, conv_weight, log_gate, write_rate, norm_gain):
    weight = conv_weight.astype(jnp.float32)
    padded = jnp.concatenate([jnp.zeros((KW - 1, CH), jnp.bfloat16), projected], axis=0)
    number = TOKEN_COUNT // STRETCH

    def advance(state, index):
        start = (index * STRETCH).astype(jnp.int32)
        window = lax.dynamic_slice_in_dim(padded, start, STRETCH + KW - 1, 0).astype(jnp.float32)
        summed = window[0:STRETCH] * weight[0]
        for start_displacement in range(1, KW):
            summed = summed + window[start_displacement:start_displacement + STRETCH] * weight[start_displacement]
        convolved = jax.nn.silu(summed).astype(jnp.bfloat16)
        queries, key_rows, values = head_rows(convolved)
        gates = lax.dynamic_slice_in_dim(log_gate, start, STRETCH, 1)
        rates = lax.dynamic_slice_in_dim(write_rate, start, STRETCH, 1)
        cumulative, decay_mat, fresh, carried = prepare(key_rows, values, gates, rates)
        output, written = apply_state(queries, key_rows, cumulative, decay_mat, fresh, carried, state)
        tail_decay = jnp.exp(cumulative[..., -1:] - cumulative)
        state = jnp.exp(cumulative[:, -1])[:, None, None] * state + jnp.einsum('...cd,...ce->...de', key_rows * tail_decay[..., None], written, precision=PRECISE)
        normed = normalize(output, norm_gain).astype(jnp.bfloat16)
        return (state, jnp.transpose(normed, (1, 0, 2)).reshape(STRETCH, VALUE_HEADS * DK))
    initial = jnp.zeros((VALUE_HEADS, DK, DK), jnp.float32)
    final_state, blocks = lax.scan(advance, initial, jnp.arange(number, dtype=jnp.int32))
    return blocks.reshape(TOKEN_COUNT, VALUE_HEADS * DK)
```

```python
import functools

import jax
import jax.numpy as jnp
from jax import lax
from jax.experimental import pallas as pl
from jax.experimental.pallas import tpu as pltpu
from jax.sharding import Mesh
from jax.sharding import PartitionSpec as P

DK = 128
V_GROUP = 2
KW = 4
STRETCH = 128
HALO = 8
BASE = 16
GROUP_CHANNELS = (2 + V_GROUP) * DK
ALL = ("outer", "inner", "head")
NEAR = ("inner", "head")

f32 = jnp.float32
bf16 = jnp.bfloat16


def product(left, right):
    return jnp.dot(left, right, preferred_element_type=f32)


def local_kernel(
    number, x_ref, halo_ref, weight_ref, gate_ref, rate_ref, summary_ref, out_ref, reach_ref, ext
):
    length = number * STRETCH
    ext[0:HALO] = halo_ref[...].astype(f32)
    ext[HALO:] = x_ref[...].astype(f32)
    weight = weight_ref[...].astype(f32)

    def convolved(c, segment):
        cols = slice(segment * DK, (segment + 1) * DK)
        start = c * STRETCH + HALO - (KW - 1)
        total = ext[start : start + STRETCH, cols] * weight[0:1, cols]
        for j in range(1, KW):
            total = total + ext[start + j : start + j + STRETCH, cols] * weight[j : j + 1, cols]
        half = 0.5 * total
        return (half + half * jnp.tanh(half)).astype(bf16)

    row = lax.broadcasted_iota(jnp.int32, (STRETCH, STRETCH), 0)
    col = lax.broadcasted_iota(jnp.int32, (STRETCH, STRETCH), 1)
    inside = row >= col
    below = row > col
    eye = jnp.where(row == col, 1.0, 0.0).astype(f32)

    gates = gate_ref[0]
    rates = rate_ref[0]
    units = gates.shape[0]
    lane = lax.broadcasted_iota(jnp.int32, gates.shape, 1)
    cumulative = gates
    for k in (1, 2, 4, 8, 16, 32, 64):
        cumulative = cumulative + jnp.where(lane >= k, pltpu.roll(cumulative, k, 1), 0.0)
    last = cumulative[:, STRETCH - 1 : STRETCH]
    grown = jnp.exp(cumulative)
    tail = jnp.exp(last - cumulative)
    columns = jnp.transpose(
        jnp.concatenate([cumulative, grown, rates], axis=0), (1, 0)
    )

    def column(kind, unit):
        at = kind * units + unit
        return columns[:, at : at + 1]

    queries, keys, values, key_inverse = [], [], {}, []
    lower, scores = {}, {}
    for c in range(number):
        q = convolved(c, 0)
        k = convolved(c, 1)
        queries.append(q)
        keys.append(k)
        gram = lax.dot_general(
            jnp.concatenate([k, q], axis=0), k, (((1,), (1,)), ((), ())), preferred_element_type=f32
        )
        diagonal = gram[:STRETCH] * eye
        inverse_row = lax.rsqrt(jnp.sum(diagonal, axis=0, keepdims=True) + 1e-06)
        inverse_col = lax.rsqrt(jnp.sum(diagonal, axis=1, keepdims=True) + 1e-06)
        key_inverse.append(inverse_row)
        key_gram = gram[:STRETCH] * inverse_row
        query_gram = gram[STRETCH:] * inverse_row
        for j in range(V_GROUP):
            unit = j * number + c
            values[unit] = convolved(c, 2 + j)
            spread = column(0, unit) - cumulative[unit : unit + 1]
            decay = jnp.exp(jnp.where(inside, spread, -1e30))
            lower[unit] = jnp.where(
                below, key_gram * decay * (column(2, unit) * inverse_col), 0.0
            )
            scores[unit] = (query_gram * decay).astype(bf16)

    blocks = STRETCH // BASE
    small_lane = lax.broadcasted_iota(jnp.int32, (BASE, STRETCH), 1)
    small_row = lax.broadcasted_iota(jnp.int32, (BASE, STRETCH), 0)
    owner = small_lane // BASE
    packed = []
    for unit in range(units):
        piece = lower[unit][0:BASE]
        for b in range(1, blocks):
            piece = jnp.where(owner == b, lower[unit][b * BASE : (b + 1) * BASE], piece)
        packed.append(piece)
    packed = jnp.concatenate(packed, axis=0)
    big_lane = lax.broadcasted_iota(jnp.int32, packed.shape, 1)
    group_start = (big_lane // BASE) * BASE
    start = jnp.where(small_lane % BASE == small_row, 1.0, 0.0).astype(f32)
    solved = jnp.broadcast_to(start[None], (units, BASE, STRETCH))
    for j in range(BASE - 1):
        spread_col = jnp.take_along_axis(packed, group_start + j, axis=1)
        solved = solved - spread_col.reshape(units, BASE, STRETCH) * solved[:, j : j + 1, :]

    recip = {}
    for unit in range(units):
        pieces = [jnp.where(owner == b, solved[unit], 0.0) for b in range(blocks)]
        rows_of_inverse = pieces
        size = BASE
        while size < STRETCH:
            per = size // BASE
            whole = jnp.concatenate(rows_of_inverse, axis=0).astype(bf16)
            odd = [b for b in range(blocks) if (b // per) % 2 == 1]
            crossing = []
            for b in odd:
                sibling = (b // per) - 1
                crossing.append(
                    jnp.where(
                        small_lane // size == sibling, lower[unit][b * BASE : (b + 1) * BASE], 0.0
                    )
                )
            first = product(jnp.concatenate(crossing, axis=0).astype(bf16), whole).astype(bf16)
            zero = jnp.zeros((BASE, STRETCH), bf16)
            laid = [zero] * blocks
            for i, b in enumerate(odd):
                laid[b] = first[i * BASE : (i + 1) * BASE]
            odd_rows = jnp.concatenate([rows_of_inverse[b] for b in odd], axis=0)
            second = product(odd_rows.astype(bf16), jnp.concatenate(laid, axis=0))
            updated = odd_rows - second
            rows_of_inverse = list(rows_of_inverse)
            for i, b in enumerate(odd):
                rows_of_inverse[b] = updated[i * BASE : (i + 1) * BASE]
            size *= 2
        recip[unit] = jnp.concatenate(rows_of_inverse, axis=0)

    for j in range(V_GROUP):
        joint = None
        for c in range(number):
            unit = j * number + c
            at = slice(unit, unit + 1)
            by_rate = recip[unit] * rates[at]
            fresh = product(by_rate.astype(bf16), values[unit])
            carried = product((by_rate * (grown[at] * key_inverse[c])).astype(bf16), keys[c])
            scaled = (
                jnp.transpose(keys[c].astype(f32), (1, 0)) * (key_inverse[c] * tail[at])
            ).astype(bf16)
            if joint is None:
                written = jnp.concatenate([fresh, -carried], axis=1)
                seen = jnp.concatenate(
                    [jnp.zeros((STRETCH, DK), f32), queries[c].astype(f32)], axis=1
                )
                previous = jnp.concatenate([jnp.zeros((DK, DK), f32), eye], axis=1)
            else:
                both = product(
                    jnp.concatenate([carried.astype(bf16), queries[c]], axis=0), joint.astype(bf16)
                )
                written = (
                    jnp.concatenate([fresh, jnp.zeros((STRETCH, DK), f32)], axis=1)
                    - both[:STRETCH]
                )
                seen = both[STRETCH:]
                previous = joint
            gained = product(
                jnp.concatenate([scores[unit], scaled], axis=0), written.astype(bf16)
            )
            result = seen * column(1, unit) + gained[:STRETCH]
            rows = slice(c * STRETCH, (c + 1) * STRETCH)
            cols = slice(j * DK, (j + 1) * DK)
            out_ref[rows, cols] = result[:, :DK]
            reach_ref[rows, cols] = result[:, DK:].astype(bf16)
            joint = previous * grown[at, STRETCH - 1 : STRETCH] + gained[STRETCH:]
        summary_ref[j, :, :DK] = joint[:, :DK].astype(bf16)
        summary_ref[j, :, DK:] = (joint[:, DK:] - eye).astype(bf16)


def local_stage(projected, halo, weight, gates, rates):
    length, channels = projected.shape
    key_heads = channels // GROUP_CHANNELS
    number = length // STRETCH
    heads = key_heads * V_GROUP
    units = V_GROUP * number
    return pl.pallas_call(
        functools.partial(local_kernel, number),
        grid=(key_heads,),
        in_specs=[
            pl.BlockSpec((length, GROUP_CHANNELS), lambda g: (0, g)),
            pl.BlockSpec((HALO, GROUP_CHANNELS), lambda g: (0, g)),
            pl.BlockSpec((KW, GROUP_CHANNELS), lambda g: (0, g)),
            pl.BlockSpec((1, units, STRETCH), lambda g: (g, 0, 0)),
            pl.BlockSpec((1, units, STRETCH), lambda g: (g, 0, 0)),
        ],
        out_specs=[
            pl.BlockSpec((V_GROUP, DK, 2 * DK), lambda g: (g, 0, 0)),
            pl.BlockSpec((length, V_GROUP * DK), lambda g: (0, g)),
            pl.BlockSpec((length, V_GROUP * DK), lambda g: (0, g)),
        ],
        out_shape=[
            jax.ShapeDtypeStruct((heads, DK, 2 * DK), bf16),
            jax.ShapeDtypeStruct((length, heads * DK), f32),
            jax.ShapeDtypeStruct((length, heads * DK), bf16),
        ],
        scratch_shapes=[pltpu.VMEM((HALO + length, GROUP_CHANNELS), f32)],
        compiler_params=pltpu.CompilerParams(vmem_limit_bytes=48 << 20),
        name="local_stage",
    )(
        projected,
        halo,
        weight,
        gates.reshape(key_heads, units, STRETCH),
        rates.reshape(key_heads, units, STRETCH),
    )


def chain_kernel(summary_ref, prefix_ref, total_ref):
    devices, heads = summary_ref.shape[0], summary_ref.shape[1]
    row = lax.broadcasted_iota(jnp.int32, (DK, DK), 0)
    col = lax.broadcasted_iota(jnp.int32, (DK, DK), 1)
    eye = jnp.where(row == col, 1.0, 0.0).astype(f32)
    for h in range(heads):
        joint = jnp.concatenate([jnp.zeros((DK, DK), f32), eye], axis=1)
        for d in range(devices):
            prefix_ref[d, h] = joint
            loss = summary_ref[d, h, :, DK:]
            high = joint.astype(bf16)
            low = (joint - high.astype(f32)).astype(bf16)
            joint = joint + (product(loss, high) + product(loss, low))
            joint = joint + jnp.concatenate(
                [summary_ref[d, h, :, :DK].astype(f32), jnp.zeros((DK, DK), f32)], axis=1
            )
        total_ref[h] = joint


def chain_stage(summary):
    devices, heads = summary.shape[:2]
    return pl.pallas_call(
        chain_kernel,
        out_shape=[
            jax.ShapeDtypeStruct((devices, heads, DK, 2 * DK), f32),
            jax.ShapeDtypeStruct((heads, DK, 2 * DK), f32),
        ],
        compiler_params=pltpu.CompilerParams(vmem_limit_bytes=48 << 20),
        name="chain_stage",
    )(summary)


def entry_kernel(prefix_ref, entering_ref, start_ref):
    devices, heads = prefix_ref.shape[0], prefix_ref.shape[1]
    for h in range(heads):
        entering = entering_ref[h]
        high = entering.astype(bf16)
        low = (entering - high.astype(f32)).astype(bf16)
        pair = jnp.concatenate([high, low], axis=1)
        for d in range(devices):
            both = product(prefix_ref[d, h, :, DK:].astype(bf16), pair)
            start_ref[d, h] = (
                prefix_ref[d, h, :, :DK] + (both[:, :DK] + both[:, DK:])
            ).astype(bf16)


def entry_stage(prefix, entering):
    devices, heads = prefix.shape[:2]
    return pl.pallas_call(
        entry_kernel,
        out_shape=jax.ShapeDtypeStruct((devices, heads, DK, DK), bf16),
        compiler_params=pltpu.CompilerParams(vmem_limit_bytes=48 << 20),
        name="entry_stage",
    )(prefix, entering)


def finish_kernel(local_ref, reach_ref, start_ref, gain_ref, out_ref):
    for h in range(start_ref.shape[0]):
        cols = slice(h * DK, (h + 1) * DK)
        result = local_ref[:, cols] + product(reach_ref[:, cols], start_ref[h])
        mean = jnp.mean(result * result, axis=1, keepdims=True)
        out_ref[:, cols] = (result * lax.rsqrt(mean + 1e-06) * gain_ref[...]).astype(bf16)


def finish_stage(local, reach, starts, gain):
    length, width = local.shape
    heads = starts.shape[0]
    step = 4
    return pl.pallas_call(
        finish_kernel,
        grid=(heads // step,),
        in_specs=[
            pl.BlockSpec((length, step * DK), lambda g: (0, g)),
            pl.BlockSpec((length, step * DK), lambda g: (0, g)),
            pl.BlockSpec((step, DK, DK), lambda g: (g, 0, 0)),
            pl.BlockSpec((1, DK), lambda g: (0, 0)),
        ],
        out_specs=pl.BlockSpec((length, step * DK), lambda g: (0, g)),
        out_shape=jax.ShapeDtypeStruct((length, width), bf16),
        compiler_params=pltpu.CompilerParams(vmem_limit_bytes=48 << 20),
        name="finish_stage",
    )(local, reach, starts, gain.reshape(1, DK))


def entering_state(total):
    outer = lax.axis_size("outer")
    if outer == 1:
        return jnp.zeros_like(total[..., :DK])
    if outer == 2:
        return lax.ppermute(total[..., :DK], "outer", [(0, 1)])
    everyone = lax.all_gather(total, "outer", axis=0)
    mine = lax.axis_index("outer")

    def step(i, state):
        piece = lax.dynamic_index_in_dim(everyone, i, 0, keepdims=False)
        moved = piece[..., :DK] + jnp.einsum(
            "hij,hjk->hik", piece[..., DK:], state, precision=lax.Precision.HIGHEST
        )
        return jnp.where(i < mine, moved, state)

    return lax.fori_loop(0, outer - 1, step, jnp.zeros_like(total[..., :DK]))


def per_device(projected, conv_weight, log_gate, write_rate, norm_gain):
    length = projected.shape[0]
    devices = lax.axis_size(ALL)
    parts = lax.axis_size("head")
    local_heads = log_gate.shape[0]
    width = conv_weight.shape[1]
    halo = lax.ppermute(
        projected[length - HALO :], ALL, [(i, i + 1) for i in range(devices - 1)]
    )
    both = jnp.stack([log_gate, write_rate]).reshape(2, local_heads, parts, length)
    both = jnp.moveaxis(both, 2, 0).reshape(parts, 2 * local_heads * length // DK, DK)
    taps = conv_weight.astype(f32).reshape(1, KW * width // DK, DK)
    packed = jnp.concatenate(
        [both, jnp.broadcast_to(taps, (parts,) + taps.shape[1:])], axis=1
    )
    packed = lax.all_to_all(packed, "head", 0, 0, tiled=True)
    split = both.shape[1]
    both = jnp.moveaxis(packed[:, :split].reshape(parts, 2, local_heads, length), 1, 0)
    both = both.reshape(2, parts * local_heads, length)
    weight = jnp.moveaxis(packed[:, split:].reshape(parts, KW, width), 0, 1)
    weight = weight.reshape(KW, parts * width)

    summary, local, reach = local_stage(projected, halo, weight, both[0], both[1])
    heads = summary.shape[0]
    near = lax.axis_size(NEAR)
    own = heads // near
    summary = lax.all_to_all(summary, NEAR, 0, 0, tiled=True)
    prefix, total = chain_stage(summary.reshape(near, own, DK, 2 * DK))
    starts = entry_stage(prefix, entering_state(total))
    starts = lax.all_to_all(starts.reshape(heads, DK, DK), NEAR, 0, 0, tiled=True)
    return finish_stage(local, reach, starts, norm_gain)


def solution(mesh):
    seq, head = mesh.shape["seq"], mesh.shape["head"]
    inner = max(1, 16 // head)
    while seq % inner:
        inner //= 2
    near = Mesh(mesh.devices.reshape(seq // inner, inner, head), ALL)
    in_specs = (
        P(ALL, None),
        P(None, "head"),
        P("head", ("outer", "inner")),
        P("head", ("outer", "inner")),
        P(),
    )
    return jax.shard_map(
        per_device, mesh=near, in_specs=in_specs, out_specs=P(ALL, None), check_vma=False
    )
```

```python
import functools

import jax
import jax.numpy as jnp
from jax import lax
from jax.experimental import pallas as pl
from jax.experimental.pallas import tpu as pltpu
from jax.sharding import Mesh
from jax.sharding import PartitionSpec as P

DK = 128
V_GROUP = 2
KW = 4
STRETCH = 128
HALO = 8
BASE = 16
SEGMENTS = 2 + V_GROUP
VMEM_BYTES = 56 << 20
GROUP_CHANNELS = (2 + V_GROUP) * DK
ALL = ("outer", "inner", "head")
NEAR = ("inner", "head")

f32 = jnp.float32
bf16 = jnp.bfloat16


def product(left, right):
    return jnp.dot(left, right, preferred_element_type=f32)


def extend(ext, halo_ref, x_ref, cols):
    ext[0:HALO, cols] = halo_ref[:, cols].astype(f32)
    ext[HALO:, cols] = x_ref[:, cols].astype(f32)


def convolved(ext, cols, taps, c):
    start = c * STRETCH + HALO - (KW - 1)
    total = ext[start : start + STRETCH, cols] * taps[0:1]
    for j in range(1, KW):
        total = total + ext[start + j : start + j + STRETCH, cols] * taps[j : j + 1]
    half = 0.5 * total
    return (half + half * jnp.tanh(half)).astype(bf16)


def running_sum(gates):
    lane = lax.broadcasted_iota(jnp.int32, gates.shape, 1)
    total = gates
    for k in (1, 2, 4, 8, 16, 32, 64):
        total = total + jnp.where(lane >= k, pltpu.roll(total, k, 1), 0.0)
    return total


def square_iotas():
    row = lax.broadcasted_iota(jnp.int32, (STRETCH, STRETCH), 0)
    col = lax.broadcasted_iota(jnp.int32, (STRETCH, STRETCH), 1)
    return row, col


def block_inverses(lower):
    units = len(lower)
    blocks = STRETCH // BASE
    small_lane = lax.broadcasted_iota(jnp.int32, (BASE, STRETCH), 1)
    small_row = lax.broadcasted_iota(jnp.int32, (BASE, STRETCH), 0)
    owner = small_lane // BASE
    packed = []
    for unit in range(units):
        piece = lower[unit][0:BASE]
        for b in range(1, blocks):
            piece = jnp.where(owner == b, lower[unit][b * BASE : (b + 1) * BASE], piece)
        packed.append(piece)
    packed = jnp.concatenate(packed, axis=0)
    group_start = (lax.broadcasted_iota(jnp.int32, packed.shape, 1) // BASE) * BASE
    start = jnp.where(small_lane % BASE == small_row, 1.0, 0.0).astype(f32)
    solved = jnp.broadcast_to(start[None], (units, BASE, STRETCH))
    for j in range(BASE - 1):
        spread_col = jnp.take_along_axis(packed, group_start + j, axis=1)
        solved = solved - spread_col.reshape(units, BASE, STRETCH) * solved[:, j : j + 1, :]

    rows = [
        [jnp.where(owner == b, solved[unit], 0.0) for b in range(blocks)] for unit in range(units)
    ]
    size = BASE
    while size < STRETCH:
        per = size // BASE
        odd = [b for b in range(blocks) if (b // per) % 2 == 1]
        firsts = []
        for unit in range(units):
            crossing = [
                jnp.where(
                    small_lane // size == (b // per) - 1,
                    lower[unit][b * BASE : (b + 1) * BASE],
                    0.0,
                )
                for b in odd
            ]
            firsts.append(
                product(
                    jnp.concatenate(crossing, axis=0).astype(bf16),
                    jnp.concatenate(rows[unit], axis=0).astype(bf16),
                ).astype(bf16)
            )
        for unit in range(units):
            laid = [jnp.zeros((BASE, STRETCH), bf16)] * blocks
            for i, b in enumerate(odd):
                laid[b] = firsts[unit][i * BASE : (i + 1) * BASE]
            odd_rows = jnp.concatenate([rows[unit][b] for b in odd], axis=0)
            updated = odd_rows - product(odd_rows.astype(bf16), jnp.concatenate(laid, axis=0))
            for i, b in enumerate(odd):
                rows[unit][b] = updated[i * BASE : (i + 1) * BASE]
        size *= 2
    return [jnp.concatenate(rows[unit], axis=0) for unit in range(units)]


def pack_kernel(parts, at_ref, x_ref, gate_ref, rate_ref, taps_ref, packed_ref, halo_ref):
    heads = gate_ref.shape[0]
    length = gate_ref.shape[1] // parts
    number = length // STRETCH
    segments = taps_ref.shape[1] // DK
    halo_ref[...] = x_ref[...]
    for i in range(packed_ref.shape[0]):
        part = at_ref[i]
        for c in range(number):
            lanes = pl.ds(pl.multiple_of(part * length + c * STRETCH, STRETCH), STRETCH)
            rows = slice(c * heads, (c + 1) * heads)
            packed_ref[i, rows] = gate_ref[:, lanes]
            rows = slice((number + c) * heads, (number + c + 1) * heads)
            packed_ref[i, rows] = rate_ref[:, lanes]
        base = 2 * number * heads
        for segment in range(segments):
            rows = slice(base + segment * KW, base + (segment + 1) * KW)
            packed_ref[i, rows] = taps_ref[:, segment * DK : (segment + 1) * DK].astype(f32)


def pack_stage(order, parts, projected, log_gate, write_rate, conv_weight):
    length, channels = projected.shape
    heads = log_gate.shape[0]
    rows = 2 * (length // STRETCH) * heads + conv_weight.shape[1] // DK * KW
    count = order.shape[0]
    whole = lambda shape: pl.BlockSpec(shape, lambda i, at: (0,) * len(shape))
    return pl.pallas_call(
        functools.partial(pack_kernel, parts),
        grid_spec=pltpu.PrefetchScalarGridSpec(
            num_scalar_prefetch=1,
            grid=(1,),
            in_specs=[
                pl.BlockSpec((HALO, channels), lambda i, at: (length // HALO - 1, 0)),
                whole(log_gate.shape),
                whole(write_rate.shape),
                whole(conv_weight.shape),
            ],
            out_specs=[whole((count, rows, DK)), whole((HALO, channels))],
        ),
        out_shape=[
            jax.ShapeDtypeStruct((count, rows, DK), f32),
            jax.ShapeDtypeStruct((HALO, channels), bf16),
        ],
        name="pack_stage",
    )(order, projected, log_gate, write_rate, conv_weight)


def local_kernel(number, into, part_ref, x_ref, halo_ref, pack_ref, *refs):
    summary_ref, written_ref, joint_ref, key_ref, norm_ref, ext = refs[into:]
    key_heads = key_ref.shape[1] // DK
    heads = key_heads * V_GROUP
    units = heads * number
    row, col = square_iotas()
    below = row > col
    eye = jnp.where(row == col, 1.0, 0.0).astype(f32)

    rates = pack_ref[0, units : 2 * units]
    cumulative = running_sum(pack_ref[0, 0:units])
    grown = jnp.exp(cumulative)
    tail = jnp.exp(cumulative[:, STRETCH - 1 : STRETCH] - cumulative)
    columns = jnp.transpose(jnp.concatenate([cumulative, rates], axis=0), (1, 0))
    where = [(c, g) for g in range(key_heads) for c in range(number)]

    def units_of(c, g):
        return [(j, c * heads + g * V_GROUP + j) for j in range(V_GROUP)]

    def channels(c, g, kind):
        segment = g * SEGMENTS + kind
        cols = slice(segment * DK, (segment + 1) * DK)
        if c == 0:
            extend(ext, halo_ref, x_ref, cols)
        at = 2 * units + segment * KW
        return convolved(ext, cols, pack_ref[0, at : at + KW], c)

    keys, inverses, lower = {}, {}, [None] * units
    for c, g in where:
        k = channels(c, g, 1)
        keys[c, g] = k
        key_ref[c * STRETCH : (c + 1) * STRETCH, g * DK : (g + 1) * DK] = k
        gram = lax.dot_general(k, k, (((1,), (1,)), ((), ())), preferred_element_type=f32)
        diagonal = gram * eye
        inverse_row = lax.rsqrt(jnp.sum(diagonal, axis=0, keepdims=True) + 1e-06)
        inverse_col = lax.rsqrt(jnp.sum(diagonal, axis=1, keepdims=True) + 1e-06)
        inverses[c, g] = inverse_row
        norm_ref[g, c : c + 1] = inverse_row
        gram = gram * inverse_row
        for j, unit in units_of(c, g):
            spread = columns[:, unit : unit + 1] - cumulative[unit : unit + 1]
            decay = jnp.exp(jnp.where(below, spread, -1e30))
            lower[unit] = gram * decay * (columns[:, units + unit : units + unit + 1] * inverse_col)

    solved = block_inverses(lower)

    fresh, carried, scaled = [None] * units, [None] * units, [None] * units
    for c, g in where:
        turned = jnp.transpose(keys[c, g].astype(f32), (1, 0)) * inverses[c, g]
        for j, unit in units_of(c, g):
            at = slice(unit, unit + 1)
            by_rate = solved[unit] * rates[at]
            fresh[unit] = product(by_rate.astype(bf16), channels(c, g, 2 + j))
            by_rate = by_rate * (grown[at] * inverses[c, g])
            carried[unit] = product(by_rate.astype(bf16), keys[c, g])
            scaled[unit] = (turned * tail[at]).astype(bf16)

    nothing = jnp.zeros((STRETCH, DK), f32)
    joint = [jnp.concatenate([jnp.zeros((DK, DK), f32), eye], axis=1)] * heads
    for c in range(number):
        for head in range(heads):
            unit = c * heads + head
            if c == 0:
                written = jnp.concatenate([fresh[unit], -carried[unit]], axis=1)
            else:
                start = joint[head].astype(bf16)
                joint_ref[c, head] = start
                written = jnp.concatenate([fresh[unit], nothing], axis=1) - product(
                    carried[unit].astype(bf16), start
                )
            written = written.astype(bf16)
            written_ref[c, head] = written
            decay = grown[unit : unit + 1, STRETCH - 1 : STRETCH]
            joint[head] = joint[head] * decay + product(scaled[unit], written)
    for head in range(heads):
        summary_ref[head, :, :DK] = joint[head][:, :DK].astype(bf16)
        summary_ref[head, :, DK:] = (joint[head][:, DK:] - eye).astype(bf16)


def pack_row(pack, index):
    return pl.BlockSpec((1,) + pack.shape[1:], lambda i, part: (index, 0, 0))


def local_stage(part, parts, projected, halo, packs, index, into=()):
    length, channels = projected.shape
    number = length // STRETCH
    width = channels // parts
    all_key_heads = channels // GROUP_CHANNELS
    all_heads = all_key_heads * V_GROUP
    key_heads = all_key_heads // parts
    heads = all_heads // parts
    per_unit = pl.BlockSpec((number, heads, STRETCH, 2 * DK), lambda i, part: (0, part[0], 0, 0))
    inputs = (part, projected, halo, packs)
    return pl.pallas_call(
        functools.partial(local_kernel, number, len(into)),
        grid_spec=pltpu.PrefetchScalarGridSpec(
            num_scalar_prefetch=1,
            grid=(1,),
            in_specs=[
                pl.BlockSpec((length, width), lambda i, part: (0, part[0])),
                pl.BlockSpec((HALO, width), lambda i, part: (0, part[0])),
                pack_row(packs, index),
            ]
            + [pl.BlockSpec(memory_space=pl.ANY)] * len(into),
            out_specs=[
                pl.BlockSpec((heads, DK, 2 * DK), lambda i, part: (part[0], 0, 0)),
                per_unit,
                per_unit,
                pl.BlockSpec((length, key_heads * DK), lambda i, part: (0, part[0])),
                pl.BlockSpec((key_heads, number, STRETCH), lambda i, part: (part[0], 0, 0)),
            ],
            scratch_shapes=[pltpu.VMEM((HALO + length, width), f32)],
        ),
        out_shape=[
            jax.ShapeDtypeStruct((all_heads, DK, 2 * DK), bf16),
            jax.ShapeDtypeStruct((number, all_heads, STRETCH, 2 * DK), bf16),
            jax.ShapeDtypeStruct((number, all_heads, STRETCH, 2 * DK), bf16),
            jax.ShapeDtypeStruct((length, all_key_heads * DK), bf16),
            jax.ShapeDtypeStruct((all_key_heads, number, STRETCH), f32),
        ],
        input_output_aliases={len(inputs) + i: i for i in range(len(into))},
        compiler_params=pltpu.CompilerParams(vmem_limit_bytes=VMEM_BYTES),
        name="local_stage",
    )(*inputs, *into)


def reading_kernel(number, part_ref, *refs):
    key_heads = refs[-3].shape[1] // (V_GROUP * DK)
    x_refs, halo_refs = refs[:key_heads], refs[key_heads : 2 * key_heads]
    pack_ref, key_ref, norm_ref, written_ref, joint_ref = refs[2 * key_heads : 2 * key_heads + 5]
    out_ref, reach_ref, ext = refs[-3:]
    heads = key_heads * V_GROUP
    units = heads * number
    row, col = square_iotas()
    inside = row >= col
    cumulative = running_sum(pack_ref[0, 0:units])
    columns = jnp.transpose(cumulative, (1, 0))
    whole = slice(0, DK)
    for g in range(key_heads):
        extend(ext.at[g], halo_refs[g], x_refs[g], whole)
        at = 2 * units + g * SEGMENTS * KW
        for c in range(number):
            rows = slice(c * STRETCH, (c + 1) * STRETCH)
            query = convolved(ext.at[g], whole, pack_ref[0, at : at + KW], c)
            gram = lax.dot_general(
                query,
                key_ref[rows, g * DK : (g + 1) * DK],
                (((1,), (1,)), ((), ())),
                preferred_element_type=f32,
            )
            gram = gram * norm_ref[g, c : c + 1]
            for j in range(V_GROUP):
                head = g * V_GROUP + j
                unit = c * heads + head
                sum_here = columns[:, unit : unit + 1]
                decay = jnp.exp(jnp.where(inside, sum_here - cumulative[unit : unit + 1], -1e30))
                result = product((gram * decay).astype(bf16), written_ref[c, head])
                grown = jnp.exp(sum_here)
                cols = slice(head * DK, (head + 1) * DK)
                if c == 0:
                    reached = result[:, DK:] + grown * query.astype(f32)
                else:
                    result = result + grown * product(query, joint_ref[c, head])
                    reached = result[:, DK:]
                out_ref[rows, cols] = result[:, :DK]
                reach_ref[rows, cols] = reached.astype(bf16)


def reading_stage(part, parts, projected, halo, packs, index, kept, into=()):
    written, joints, keys, norms = kept
    length, channels = projected.shape
    number = length // STRETCH
    all_key_heads = channels // GROUP_CHANNELS
    key_heads = all_key_heads // parts
    heads = key_heads * V_GROUP
    per_unit = pl.BlockSpec((number, heads, STRETCH, 2 * DK), lambda i, part: (0, part[0], 0, 0))
    per_head = pl.BlockSpec((length, heads * DK), lambda i, part: (0, part[0]))
    query = lambda g: lambda i, part: (0, (part[0] * key_heads + g) * SEGMENTS)
    inputs = (part,) + (projected,) * key_heads + (halo,) * key_heads
    inputs += (packs, keys, norms, written, joints)
    width = all_key_heads * V_GROUP * DK
    return pl.pallas_call(
        functools.partial(reading_kernel, number),
        grid_spec=pltpu.PrefetchScalarGridSpec(
            num_scalar_prefetch=1,
            grid=(1,),
            in_specs=[pl.BlockSpec((length, DK), query(g)) for g in range(key_heads)]
            + [pl.BlockSpec((HALO, DK), query(g)) for g in range(key_heads)]
            + [
                pack_row(packs, index),
                pl.BlockSpec((length, key_heads * DK), lambda i, part: (0, part[0])),
                pl.BlockSpec((key_heads, number, STRETCH), lambda i, part: (part[0], 0, 0)),
                per_unit,
                per_unit,
            ]
            + [pl.BlockSpec(memory_space=pl.ANY)] * len(into),
            out_specs=[per_head, per_head],
            scratch_shapes=[pltpu.VMEM((key_heads, HALO + length, DK), f32)],
        ),
        out_shape=[
            jax.ShapeDtypeStruct((length, width), f32),
            jax.ShapeDtypeStruct((length, width), bf16),
        ],
        input_output_aliases={len(inputs) + i: i for i in range(len(into))},
        compiler_params=pltpu.CompilerParams(vmem_limit_bytes=VMEM_BYTES),
        name="reading_stage",
    )(*inputs, *into)


def chain_kernel(summary_ref, prefix_ref, total_ref):
    devices, heads = summary_ref.shape[0], summary_ref.shape[1]
    row = lax.broadcasted_iota(jnp.int32, (DK, DK), 0)
    col = lax.broadcasted_iota(jnp.int32, (DK, DK), 1)
    eye = jnp.where(row == col, 1.0, 0.0).astype(f32)
    for h in range(heads):
        joint = jnp.concatenate([jnp.zeros((DK, DK), f32), eye], axis=1)
        for d in range(devices):
            prefix_ref[d, h] = joint
            loss = summary_ref[d, h, :, DK:]
            high = joint.astype(bf16)
            low = (joint - high.astype(f32)).astype(bf16)
            joint = joint + (product(loss, high) + product(loss, low))
            joint = joint + jnp.concatenate(
                [summary_ref[d, h, :, :DK].astype(f32), jnp.zeros((DK, DK), f32)], axis=1
            )
        total_ref[h] = joint


def chain_stage(summary):
    devices, heads = summary.shape[:2]
    return pl.pallas_call(
        chain_kernel,
        out_shape=[
            jax.ShapeDtypeStruct((devices, heads, DK, 2 * DK), f32),
            jax.ShapeDtypeStruct((heads, DK, 2 * DK), f32),
        ],
        compiler_params=pltpu.CompilerParams(vmem_limit_bytes=48 << 20),
        name="chain_stage",
    )(summary)


def entry_kernel(prefix_ref, entering_ref, start_ref):
    devices, heads = prefix_ref.shape[0], prefix_ref.shape[1]
    for h in range(heads):
        entering = entering_ref[h]
        high = entering.astype(bf16)
        low = (entering - high.astype(f32)).astype(bf16)
        pair = jnp.concatenate([high, low], axis=1)
        for d in range(devices):
            both = product(prefix_ref[d, h, :, DK:].astype(bf16), pair)
            start_ref[d, h] = (
                prefix_ref[d, h, :, :DK] + (both[:, :DK] + both[:, DK:])
            ).astype(bf16)


def entry_stage(prefix, entering):
    devices, heads = prefix.shape[:2]
    return pl.pallas_call(
        entry_kernel,
        out_shape=jax.ShapeDtypeStruct((devices, heads, DK, DK), bf16),
        compiler_params=pltpu.CompilerParams(vmem_limit_bytes=48 << 20),
        name="entry_stage",
    )(prefix, entering)


def finish_kernel(local_ref, reach_ref, start_ref, gain_ref, out_ref):
    for h in range(start_ref.shape[0]):
        cols = slice(h * DK, (h + 1) * DK)
        result = local_ref[:, cols] + product(reach_ref[:, cols], start_ref[h])
        mean = jnp.mean(result * result, axis=1, keepdims=True)
        out_ref[:, cols] = (result * lax.rsqrt(mean + 1e-06) * gain_ref[...]).astype(bf16)


def finish_stage(local, reach, starts, gain):
    length, width = local.shape
    heads = starts.shape[0]
    step = 4
    return pl.pallas_call(
        finish_kernel,
        grid=(heads // step,),
        in_specs=[
            pl.BlockSpec((length, step * DK), lambda g: (0, g)),
            pl.BlockSpec((length, step * DK), lambda g: (0, g)),
            pl.BlockSpec((step, DK, DK), lambda g: (g, 0, 0)),
            pl.BlockSpec((1, DK), lambda g: (0, 0)),
        ],
        out_specs=pl.BlockSpec((length, step * DK), lambda g: (0, g)),
        out_shape=jax.ShapeDtypeStruct((length, width), bf16),
        compiler_params=pltpu.CompilerParams(vmem_limit_bytes=48 << 20),
        name="finish_stage",
    )(local, reach, starts, gain.reshape(1, DK))


def entering_state(total):
    outer = lax.axis_size("outer")
    if outer == 1:
        return jnp.zeros_like(total[..., :DK])
    if outer == 2:
        return lax.ppermute(total[..., :DK], "outer", [(0, 1)])
    everyone = lax.all_gather(total, "outer", axis=0)
    mine = lax.axis_index("outer")

    def step(i, state):
        piece = lax.dynamic_index_in_dim(everyone, i, 0, keepdims=False)
        moved = piece[..., :DK] + jnp.einsum(
            "hij,hjk->hik", piece[..., DK:], state, precision=lax.Precision.HIGHEST
        )
        return jnp.where(i < mine, moved, state)

    return lax.fori_loop(0, outer - 1, step, jnp.zeros_like(total[..., :DK]))


def per_device(projected, conv_weight, log_gate, write_rate, norm_gain):
    devices = lax.axis_size(ALL)
    parts = lax.axis_size("head")
    route = [(i, i + 1) for i in range(devices - 1)]
    mine = lax.axis_index("head").astype(jnp.int32)
    if parts == 2:
        order = jnp.stack([mine, 1 - mine])
        packs, tail = pack_stage(order, parts, projected, log_gate, write_rate, conv_weight)
        halo = lax.ppermute(tail, ALL, route)
        theirs = lax.ppermute(packs[1:], "head", [(0, 1), (1, 0)])
        pieces = [(order[:1], packs, 0), (order[1:], theirs, 0)]
    else:
        order = jnp.arange(parts, dtype=jnp.int32)
        packs, tail = pack_stage(order, parts, projected, log_gate, write_rate, conv_weight)
        halo = lax.ppermute(tail, ALL, route)
        packs = lax.all_to_all(packs, "head", 0, 0, tiled=True)
        pieces = [(order[p : p + 1], packs, p) for p in range(parts)]

    made = ()
    for part, pack, index in pieces:
        made = local_stage(part, parts, projected, halo, pack, index, made)
    summary, *kept = made
    heads = summary.shape[0]
    near = lax.axis_size(NEAR)
    own = heads // near
    summary = lax.all_to_all(summary, NEAR, 0, 0, tiled=True)
    read = ()
    early = max(1, len(pieces) // 2)
    for part, pack, index in pieces[:early]:
        read = reading_stage(part, parts, projected, halo, pack, index, kept, read)
    summary, read = lax.optimization_barrier((summary, read))
    prefix, total = chain_stage(summary.reshape(near, own, DK, 2 * DK))
    starts = entry_stage(prefix, entering_state(total))
    starts, read = lax.optimization_barrier((starts, read))
    starts = lax.all_to_all(starts.reshape(heads, DK, DK), NEAR, 0, 0, tiled=True)
    for part, pack, index in pieces[early:]:
        read = reading_stage(part, parts, projected, halo, pack, index, kept, read)
    local, reach = read
    return finish_stage(local, reach, starts, norm_gain)


def solution(mesh):
    seq, head = mesh.shape["seq"], mesh.shape["head"]
    inner = max(1, 16 // head)
    while seq % inner:
        inner //= 2
    near = Mesh(mesh.devices.reshape(seq // inner, inner, head), ALL)
    in_specs = (
        P(ALL, None),
        P(None, "head"),
        P("head", ("outer", "inner")),
        P("head", ("outer", "inner")),
        P(),
    )
    return jax.shard_map(
        per_device, mesh=near, in_specs=in_specs, out_specs=P(ALL, None), check_vma=False
    )
```

```python
import functools

import jax
import jax.numpy as jnp
from jax import lax
from jax.experimental import pallas as pl
from jax.experimental.pallas import tpu as pltpu
from jax.sharding import Mesh
from jax.sharding import PartitionSpec as P

DK = 128
V_GROUP = 2
KW = 4
STRETCH = 128
HALO = 8
BASE = 16
SEGMENTS = 2 + V_GROUP
GROUP_CHANNELS = (2 + V_GROUP) * DK
ALL = ("outer", "inner", "head")
NEAR = ("inner", "head")

f32 = jnp.float32
bf16 = jnp.bfloat16


VMEM = pl.BlockSpec(memory_space=pltpu.VMEM)
SMEM = pl.BlockSpec(memory_space=pltpu.SMEM)
FAR = pl.BlockSpec(memory_space=pltpu.HBM)


def near(array):
    return pltpu.with_memory_space_constraint(array, pltpu.VMEM)


def far(array):
    return pltpu.with_memory_space_constraint(array, pltpu.HBM)


def product(left, right):
    return jnp.dot(left, right, preferred_element_type=f32)


def part_at(first, step, parts):
    return lax.rem(first + step, parts)


def lanes_of(start):
    return pl.ds(pl.multiple_of(start, DK), DK)


def convolved(ext, cols, taps, c):
    start = c * STRETCH + HALO - (KW - 1)
    total = ext[start : start + STRETCH, cols] * taps[0:1]
    for j in range(1, KW):
        total = total + ext[start + j : start + j + STRETCH, cols] * taps[j : j + 1]
    half = 0.5 * total
    return (half + half * jnp.tanh(half)).astype(bf16)


def running_sum(gates):
    lane = lax.broadcasted_iota(jnp.int32, gates.shape, 1)
    total = gates
    for k in (1, 2, 4, 8, 16, 32, 64):
        total = total + jnp.where(lane >= k, pltpu.roll(total, k, 1), 0.0)
    return total


def square_iotas():
    row = lax.broadcasted_iota(jnp.int32, (STRETCH, STRETCH), 0)
    col = lax.broadcasted_iota(jnp.int32, (STRETCH, STRETCH), 1)
    return row, col


def block_inverses(lower):
    units = len(lower)
    blocks = STRETCH // BASE
    small_lane = lax.broadcasted_iota(jnp.int32, (BASE, STRETCH), 1)
    small_row = lax.broadcasted_iota(jnp.int32, (BASE, STRETCH), 0)
    owner = small_lane // BASE
    packed = []
    for unit in range(units):
        piece = lower[unit][0:BASE]
        for b in range(1, blocks):
            piece = jnp.where(owner == b, lower[unit][b * BASE : (b + 1) * BASE], piece)
        packed.append(piece)
    packed = jnp.concatenate(packed, axis=0)
    group_start = (lax.broadcasted_iota(jnp.int32, packed.shape, 1) // BASE) * BASE
    start = jnp.where(small_lane % BASE == small_row, 1.0, 0.0).astype(f32)
    solved = jnp.broadcast_to(start[None], (units, BASE, STRETCH))
    for j in range(BASE - 1):
        spread_col = jnp.take_along_axis(packed, group_start + j, axis=1)
        solved = solved - spread_col.reshape(units, BASE, STRETCH) * solved[:, j : j + 1, :]

    rows = [
        [jnp.where(owner == b, solved[unit], 0.0) for b in range(blocks)] for unit in range(units)
    ]
    size = BASE
    while size < STRETCH:
        per = size // BASE
        odd = [b for b in range(blocks) if (b // per) % 2 == 1]
        firsts = []
        for unit in range(units):
            crossing = [
                jnp.where(
                    small_lane // size == (b // per) - 1,
                    lower[unit][b * BASE : (b + 1) * BASE],
                    0.0,
                )
                for b in odd
            ]
            firsts.append(
                product(
                    jnp.concatenate(crossing, axis=0).astype(bf16),
                    jnp.concatenate(rows[unit], axis=0).astype(bf16),
                ).astype(bf16)
            )
        for unit in range(units):
            laid = [jnp.zeros((BASE, STRETCH), bf16)] * blocks
            for i, b in enumerate(odd):
                laid[b] = firsts[unit][i * BASE : (i + 1) * BASE]
            odd_rows = jnp.concatenate([rows[unit][b] for b in odd], axis=0)
            updated = odd_rows - product(odd_rows.astype(bf16), jnp.concatenate(laid, axis=0))
            for i, b in enumerate(odd):
                rows[unit][b] = updated[i * BASE : (i + 1) * BASE]
        size *= 2
    return [jnp.concatenate(rows[unit], axis=0) for unit in range(units)]


def pack_kernel(parts, first_ref, x_ref, gate_ref, rate_ref, taps_ref, halo_ref, *pack_refs):
    heads = gate_ref.shape[0]
    length = gate_ref.shape[1] // parts
    number = length // STRETCH
    segments = taps_ref.shape[1] // DK
    halo_ref[...] = x_ref[...]
    base = 2 * number * heads
    slots = [(ref, i) for ref in pack_refs for i in range(ref.shape[0])]
    for step, (ref, i) in enumerate(slots):
        first = part_at(first_ref[0], step, parts) * length
        for c in range(number):
            lanes = lanes_of(first + c * STRETCH)
            ref[i, c * heads : (c + 1) * heads] = gate_ref[:, lanes]
            ref[i, (number + c) * heads : (number + c + 1) * heads] = rate_ref[:, lanes]
        for segment in range(segments):
            rows = slice(base + segment * KW, base + (segment + 1) * KW)
            ref[i, rows] = taps_ref[:, segment * DK : (segment + 1) * DK].astype(f32)


def pack_stage(first, stacks, parts, projected, log_gate, write_rate, conv_weight):
    length, channels = projected.shape
    heads = log_gate.shape[0]
    rows = 2 * (length // STRETCH) * heads + conv_weight.shape[1] // DK * KW
    whole = lambda array: pl.BlockSpec(array.shape, lambda i: (0, 0))
    return pl.pallas_call(
        functools.partial(pack_kernel, parts),
        grid=(1,),
        in_specs=[
            SMEM,
            pl.BlockSpec((HALO, channels), lambda i: (length // HALO - 1, 0)),
            whole(log_gate),
            whole(write_rate),
            whole(conv_weight),
        ],
        out_specs=[VMEM] * (1 + len(stacks)),
        out_shape=[pltpu.VMEM((HALO, channels), bf16)]
        + [pltpu.VMEM((count, rows, DK), f32) for count in stacks],
        compiler_params=pltpu.CompilerParams(vmem_limit_bytes=2 << 20),
        name="pack_stage",
    )(first, far(projected), far(log_gate), far(write_rate), far(conv_weight))


def local_kernel(number, parts, stacks, first_ref, x_ref, halo_ref, *refs):
    pack_refs, refs = refs[: len(stacks)], refs[len(stacks) :]
    summary_out, written_out, joint_out, key_out, norm_ref = refs[:5]
    pack, blocks, ext, summaries, writtens, joints, keys_held, in_sems, out_sems = refs[5:]
    step = pl.program_id(0)
    slot = lax.rem(step, 2)
    part = part_at(first_ref[0], step, parts)
    key_heads = norm_ref.shape[1]
    width = key_heads * GROUP_CHANNELS
    heads = key_heads * V_GROUP
    units = heads * number
    block, summary_ref, written_ref = blocks.at[slot], summaries.at[slot], writtens.at[slot]
    joint_ref, key_ref = joints.at[slot], keys_held.at[slot]

    def arriving(at):
        here = lax.rem(at, 2)
        base = part_at(first_ref[0], at, parts) * width
        used = (SEGMENTS - 1) * DK
        copies = []
        for g in range(key_heads):
            source = pl.ds(pl.multiple_of(base + (g * SEGMENTS + 1) * DK, DK), used)
            target = pl.ds((g * SEGMENTS + 1) * DK, used)
            copies.append(
                pltpu.make_async_copy(
                    x_ref.at[:, source], blocks.at[here, :, target], in_sems.at[here, g]
                )
            )
        return copies

    def leaving(at):
        here = lax.rem(at, 2)
        place = pl.ds(part_at(first_ref[0], at, parts) * heads, heads)
        pairs = [(keys_held.at[here], key_out.at[at]), (summaries.at[here], summary_out.at[place])]
        pairs += [(writtens.at[here, c], written_out.at[at, c]) for c in range(number)]
        pairs += [(joints.at[here, c - 1], joint_out.at[at, c]) for c in range(1, number)]
        return [
            pltpu.make_async_copy(source, target, out_sems.at[here, i])
            for i, (source, target) in enumerate(pairs)
        ]

    @pl.when(step == 0)
    def _():
        for copy in arriving(step):
            copy.start()

    @pl.when(step + 1 < pl.num_programs(0))
    def _():
        for copy in arriving(step + 1):
            copy.start()

    coming, going = arriving(step), leaving(step)
    entries = [(ref, i) for ref in pack_refs for i in range(ref.shape[0])]
    for n, (ref, i) in enumerate(entries):

        @pl.when(step == n)
        def _():
            pack[...] = ref[i]

    row, col = square_iotas()
    below = row > col
    eye = jnp.where(row == col, 1.0, 0.0).astype(f32)

    rates = pack[units : 2 * units]
    cumulative = running_sum(pack[0:units])
    grown = jnp.exp(cumulative)
    tail = jnp.exp(cumulative[:, STRETCH - 1 : STRETCH] - cumulative)
    columns = jnp.transpose(jnp.concatenate([cumulative, rates], axis=0), (1, 0))
    where = [(c, g) for g in range(key_heads) for c in range(number)]

    def units_of(c, g):
        return [(j, c * heads + g * V_GROUP + j) for j in range(V_GROUP)]

    def channels(c, g, kind):
        segment = g * SEGMENTS + kind
        cols = slice(segment * DK, (segment + 1) * DK)
        if c == 0:
            ext[0:HALO, cols] = halo_ref[:, lanes_of(part * width + segment * DK)].astype(f32)
            ext[HALO:, cols] = block[:, cols].astype(f32)
        at = 2 * units + segment * KW
        return convolved(ext, cols, pack[at : at + KW], c)

    keys, inverses, lower = {}, {}, [None] * units
    for c, g in where:
        if c == 0:
            coming[g].wait()
        k = channels(c, g, 1)
        keys[c, g] = k
        key_ref[c * STRETCH : (c + 1) * STRETCH, g * DK : (g + 1) * DK] = k
        gram = lax.dot_general(k, k, (((1,), (1,)), ((), ())), preferred_element_type=f32)
        diagonal = gram * eye
        inverse_row = lax.rsqrt(jnp.sum(diagonal, axis=0, keepdims=True) + 1e-06)
        inverse_col = lax.rsqrt(jnp.sum(diagonal, axis=1, keepdims=True) + 1e-06)
        inverses[c, g] = inverse_row
        norm_ref[0, g, c : c + 1] = inverse_row
        gram = gram * inverse_row
        for j, unit in units_of(c, g):
            spread = columns[:, unit : unit + 1] - cumulative[unit : unit + 1]
            decay = jnp.exp(jnp.where(below, spread, -1e30))
            lower[unit] = gram * decay * (columns[:, units + unit : units + unit + 1] * inverse_col)

    going[0].start()
    solved = block_inverses(lower)

    fresh, carried, scaled = [None] * units, [None] * units, [None] * units
    for c, g in where:
        turned = jnp.transpose(keys[c, g].astype(f32), (1, 0)) * inverses[c, g]
        for j, unit in units_of(c, g):
            at = slice(unit, unit + 1)
            by_rate = solved[unit] * rates[at]
            fresh[unit] = product(by_rate.astype(bf16), channels(c, g, 2 + j))
            by_rate = by_rate * (grown[at] * inverses[c, g])
            carried[unit] = product(by_rate.astype(bf16), keys[c, g])
            scaled[unit] = (turned * tail[at]).astype(bf16)

    nothing = jnp.zeros((STRETCH, DK), f32)
    joint = [jnp.concatenate([jnp.zeros((DK, DK), f32), eye], axis=1)] * heads
    for c in range(number):
        for head in range(heads):
            unit = c * heads + head
            if c == 0:
                written = jnp.concatenate([fresh[unit], -carried[unit]], axis=1)
            else:
                start = joint[head].astype(bf16)
                joint_ref[c - 1, head] = start
                written = jnp.concatenate([fresh[unit], nothing], axis=1) - product(
                    carried[unit].astype(bf16), start
                )
            written = written.astype(bf16)
            written_ref[c, head] = written
            decay = grown[unit : unit + 1, STRETCH - 1 : STRETCH]
            joint[head] = joint[head] * decay + product(scaled[unit], written)
        going[2 + c].start()
        if c > 0:
            going[1 + number + c].start()
    for head in range(heads):
        summary_ref[head, :, :DK] = joint[head][:, :DK].astype(bf16)
        summary_ref[head, :, DK:] = (joint[head][:, DK:] - eye).astype(bf16)
    going[1].start()

    @pl.when(step > 0)
    def _():
        for copy in leaving(step - 1):
            copy.wait()

    @pl.when(step + 1 == pl.num_programs(0))
    def _():
        for copy in going:
            copy.wait()


def local_stage(first, parts, projected, halo, packs):
    length, channels = projected.shape
    number = length // STRETCH
    width = channels // parts
    key_heads = width // GROUP_CHANNELS
    heads = key_heads * V_GROUP
    per_unit = (number, heads, STRETCH, 2 * DK)
    later = (max(1, number - 1), heads, STRETCH, 2 * DK)
    return pl.pallas_call(
        functools.partial(local_kernel, number, parts, tuple(p.shape[0] for p in packs)),
        grid=(parts,),
        in_specs=[SMEM, FAR] + [VMEM] * (1 + len(packs)),
        out_specs=[FAR] * 4
        + [pl.BlockSpec((1, key_heads, number, STRETCH), lambda p: (p, 0, 0, 0))],
        out_shape=[
            pltpu.HBM((heads * parts, DK, 2 * DK), bf16),
            pltpu.HBM((parts,) + per_unit, bf16),
            pltpu.HBM((parts,) + per_unit, bf16),
            pltpu.HBM((parts, length, key_heads * DK), bf16),
            jax.ShapeDtypeStruct((parts, key_heads, number, STRETCH), f32),
        ],
        scratch_shapes=[
            pltpu.VMEM(packs[0].shape[1:], f32),
            pltpu.VMEM((2, length, width), bf16),
            pltpu.VMEM((HALO + length, width), f32),
            pltpu.VMEM((2, heads, DK, 2 * DK), bf16),
            pltpu.VMEM((2,) + per_unit, bf16),
            pltpu.VMEM((2,) + later, bf16),
            pltpu.VMEM((2, length, key_heads * DK), bf16),
            pltpu.SemaphoreType.DMA((2, key_heads)),
            pltpu.SemaphoreType.DMA((2, 2 * number + 1)),
        ],
        compiler_params=pltpu.CompilerParams(vmem_limit_bytes=44 << 20),
        name="local_stage",
    )(first, far(projected), near(halo), *(near(p) for p in packs))


def reading_kernel(number, index, first_ref, x_ref, halo_ref, pack_ref, *refs):
    written_ref, joint_ref, key_ref, norm_ref, out_ref, reach_ref, ext = refs
    heads = pl.num_programs(0) * V_GROUP
    g = pl.program_id(0)
    units = heads * number
    row, col = square_iotas()
    inside = row >= col
    gates = [
        pack_ref[index, pl.ds(c * heads + g * V_GROUP, V_GROUP)] for c in range(number)
    ]
    cumulative = running_sum(jnp.concatenate(gates, axis=0))
    columns = jnp.transpose(cumulative, (1, 0))
    ext[0:HALO] = halo_ref[...].astype(f32)
    ext[HALO:] = x_ref[...].astype(f32)
    taps = pack_ref[index, pl.ds(2 * units + g * SEGMENTS * KW, KW)]
    for c in range(number):
        rows = slice(c * STRETCH, (c + 1) * STRETCH)
        query = convolved(ext, slice(0, DK), taps, c)
        gram = lax.dot_general(
            query, key_ref[0, rows], (((1,), (1,)), ((), ())), preferred_element_type=f32
        )
        gram = gram * norm_ref[0, pl.ds(g, 1), c]
        for j in range(V_GROUP):
            unit = c * V_GROUP + j
            sum_here = columns[:, unit : unit + 1]
            decay = jnp.exp(jnp.where(inside, sum_here - cumulative[unit : unit + 1], -1e30))
            result = product((gram * decay).astype(bf16), written_ref[0, c, j])
            grown = jnp.exp(sum_here)
            if c == 0:
                reached = result[:, DK:] + grown * query.astype(f32)
            else:
                result = result + grown * product(query, joint_ref[0, c, j])
                reached = result[:, DK:]
            out_ref[j, rows] = result[:, :DK].astype(bf16)
            reach_ref[j, rows] = reached.astype(bf16)


def reading_stage(first, step, parts, projected, halo, packs, index, kept):
    length, channels = projected.shape
    number = length // STRETCH
    key_heads = channels // parts // GROUP_CHANNELS
    heads = key_heads * V_GROUP
    written, joints, keys, norms = kept
    query = lambda g, first: (0, (part_at(first[0], step, parts) * key_heads + g) * SEGMENTS)
    per_unit = pl.BlockSpec(
        (1, number, V_GROUP, STRETCH, 2 * DK), lambda g, first: (step, 0, g, 0, 0)
    )
    per_head = pl.BlockSpec((V_GROUP, length, DK), lambda g, first: (g, 0, 0))
    return pl.pallas_call(
        functools.partial(reading_kernel, number, index),
        grid_spec=pltpu.PrefetchScalarGridSpec(
            num_scalar_prefetch=1,
            grid=(key_heads,),
            in_specs=[
                pl.BlockSpec((length, DK), query),
                pl.BlockSpec((HALO, DK), query),
                pl.BlockSpec(packs.shape, lambda g, first: (0, 0, 0)),
                per_unit,
                per_unit,
                pl.BlockSpec((1, length, DK), lambda g, first: (step, 0, g)),
                pl.BlockSpec((1,) + norms.shape[1:], lambda g, first: (step, 0, 0, 0)),
            ],
            out_specs=[per_head, per_head],
            scratch_shapes=[pltpu.VMEM((HALO + length, DK), f32)],
        ),
        out_shape=[pltpu.HBM((heads, length, DK), bf16)] * 2,
        compiler_params=pltpu.CompilerParams(vmem_limit_bytes=12 << 20),
        name="reading_stage",
    )(first, far(projected), halo, packs, far(written), far(joints), far(keys), norms)


def advance(joint, loss, gain):
    high = joint.astype(bf16)
    low = (joint - high.astype(f32)).astype(bf16)
    return joint + (product(loss, high) + product(loss, low)) + gain


def chain_kernel(run, summary_ref, state_ref, loss_ref, sub_ref, total_ref):
    devices, heads = summary_ref.shape[0], summary_ref.shape[1]
    row, col = square_iotas()
    eye = jnp.where(row == col, 1.0, 0.0).astype(f32)
    nothing = jnp.zeros((DK, DK), f32)
    start = jnp.concatenate([nothing, eye], axis=1)
    for h in range(heads):
        joint = [start] * (devices // run)
        for k in range(run):
            for i in range(devices // run):
                d = i * run + k
                state_ref[d, h] = joint[i][:, :DK]
                loss_ref[d, h] = (joint[i][:, DK:] - eye).astype(bf16)
                gain = jnp.concatenate([summary_ref[d, h, :, :DK].astype(f32), nothing], axis=1)
                joint[i] = advance(joint[i], summary_ref[d, h, :, DK:], gain)
        total = joint[0]
        for i in range(devices // run):
            sub_ref[i, h] = joint[i]
            if i > 0:
                gain = jnp.concatenate([joint[i][:, :DK], nothing], axis=1)
                total = advance(total, (joint[i][:, DK:] - eye).astype(bf16), gain)
        total_ref[h] = total


def chain_stage(summary):
    devices, heads = summary.shape[:2]
    run = 4 if devices % 4 == 0 else devices
    return pl.pallas_call(
        functools.partial(chain_kernel, run),
        in_specs=[VMEM],
        out_specs=[VMEM] * 4,
        out_shape=[
            pltpu.VMEM((devices, heads, DK, DK), f32),
            pltpu.VMEM((devices, heads, DK, DK), bf16),
            pltpu.VMEM((devices // run, heads, DK, 2 * DK), f32),
            pltpu.VMEM((heads, DK, 2 * DK), f32),
        ],
        compiler_params=pltpu.CompilerParams(vmem_limit_bytes=12 << 20),
        name="chain_stage",
    )(near(summary))


def entry_kernel(state_ref, loss_ref, sub_ref, entering_ref, start_ref):
    devices, heads = state_ref.shape[0], state_ref.shape[1]
    runs = sub_ref.shape[0]
    run = devices // runs
    row, col = square_iotas()
    eye = jnp.where(row == col, 1.0, 0.0).astype(f32)
    for h in range(heads):
        entering = [entering_ref[h]]
        for i in range(runs - 1):
            loss = (sub_ref[i, h, :, DK:] - eye).astype(bf16)
            entering.append(advance(entering[i], loss, sub_ref[i, h, :, :DK]))
        for d in range(devices):
            start = advance(entering[d // run], loss_ref[d, h], state_ref[d, h])
            start_ref[d, h] = start.astype(bf16)


def entry_stage(states, losses, subs, entering):
    devices, heads = states.shape[:2]
    return pl.pallas_call(
        entry_kernel,
        in_specs=[VMEM] * 4,
        out_specs=VMEM,
        out_shape=jax.ShapeDtypeStruct((devices, heads, DK, DK), bf16),
        compiler_params=pltpu.CompilerParams(vmem_limit_bytes=12 << 20),
        name="entry_stage",
    )(states, losses, subs, near(entering))


def finish_kernel(batch, first_ref, start_ref, gain_ref, *refs):
    reads, refs = refs[:-7], refs[-7:]
    out_ref, gain, held_local, held_reach, done, in_sems, out_sems = refs
    parts = len(reads) // 2
    heads = reads[0].shape[0]
    arriving, leaving = [], []
    for p in range(parts):
        for b in range(heads // batch):
            at = pl.ds(b * batch, batch)
            into = pl.ds(p * heads + b * batch, batch)
            n = len(arriving)
            arriving.append(
                (
                    pltpu.make_async_copy(
                        reads[2 * p].at[at], held_local.at[into], in_sems.at[0, n]
                    ),
                    pltpu.make_async_copy(
                        reads[2 * p + 1].at[at], held_reach.at[into], in_sems.at[1, n]
                    ),
                )
            )
            for copy in arriving[-1]:
                copy.start()
    gain_copy = pltpu.make_async_copy(gain_ref, gain, in_sems.at[0, len(arriving)])
    gain_copy.start()
    gain_copy.wait()
    for p in range(parts):
        part = part_at(first_ref[0], p, parts)
        for b in range(heads // batch):
            n = len(leaving)
            for copy in arriving[n]:
                copy.wait()
            for k in range(batch):
                h = p * heads + b * batch + k
                start = start_ref[part * heads + b * batch + k]
                result = held_local[h].astype(f32) + product(held_reach[h], start)
                mean = jnp.mean(result * result, axis=1, keepdims=True)
                scaled = result * lax.rsqrt(mean + 1e-06) * gain[...]
                done[:, h * DK : (h + 1) * DK] = scaled.astype(bf16)
            width = batch * DK
            to = pl.ds(pl.multiple_of((part * heads + b * batch) * DK, DK), width)
            leaving.append(
                pltpu.make_async_copy(
                    done.at[:, pl.ds(n * width, width)], out_ref.at[:, to], out_sems.at[n]
                )
            )
            leaving[-1].start()
    for copy in leaving:
        copy.wait()


def finish_stage(first, reads, starts, gain):
    heads, length, _ = reads[0][0].shape
    all_heads = starts.shape[0]
    batch = 2
    return pl.pallas_call(
        functools.partial(finish_kernel, batch),
        in_specs=[SMEM, VMEM, FAR] + [FAR] * (2 * len(reads)),
        out_specs=FAR,
        out_shape=pltpu.HBM((length, all_heads * DK), bf16),
        scratch_shapes=[
            pltpu.VMEM((1, DK), f32),
            pltpu.VMEM((all_heads, length, DK), bf16),
            pltpu.VMEM((all_heads, length, DK), bf16),
            pltpu.VMEM((length, all_heads * DK), bf16),
            pltpu.SemaphoreType.DMA((2, all_heads // batch + 1)),
            pltpu.SemaphoreType.DMA((all_heads // batch,)),
        ],
        compiler_params=pltpu.CompilerParams(vmem_limit_bytes=16 << 20),
        name="finish_stage",
    )(first, near(starts), far(gain.reshape(1, DK)), *(far(a) for read in reads for a in read))


def entering_state(total):
    outer = lax.axis_size("outer")
    if outer == 1:
        return jnp.zeros_like(total[..., :DK])
    if outer == 2:
        return lax.ppermute(total[..., :DK], "outer", [(0, 1)])
    everyone = lax.all_gather(total, "outer", axis=0)
    mine = lax.axis_index("outer")

    def step(i, state):
        piece = lax.dynamic_index_in_dim(everyone, i, 0, keepdims=False)
        moved = piece[..., :DK] + jnp.einsum(
            "hij,hjk->hik", piece[..., DK:], state, precision=lax.Precision.HIGHEST
        )
        return jnp.where(i < mine, moved, state)

    return lax.fori_loop(0, outer - 1, step, jnp.zeros_like(total[..., :DK]))


def per_device(projected, conv_weight, log_gate, write_rate, norm_gain):
    devices = lax.axis_size(ALL)
    parts = lax.axis_size("head")
    route = [(i, i + 1) for i in range(devices - 1)]
    arguments = (projected, log_gate, write_rate, conv_weight)
    if parts == 2:
        first = lax.axis_index("head").astype(jnp.int32).reshape(1)
        tail, mine, theirs = pack_stage(first, (1, 1), parts, *arguments)
        halo = lax.ppermute(tail, ALL, route)
        packs = [mine, lax.ppermute(theirs, "head", [(0, 1), (1, 0)])]
    else:
        first = jnp.zeros((1,), jnp.int32)
        tail, mine = pack_stage(first, (parts,), parts, *arguments)
        halo = lax.ppermute(tail, ALL, route)
        packs = [lax.all_to_all(mine, "head", 0, 0, tiled=True)]
    entries = [(pack, i) for pack in packs for i in range(pack.shape[0])]

    summary, *kept = local_stage(first, parts, projected, halo, packs)
    heads = summary.shape[0]
    members = lax.axis_size(NEAR)
    own = heads // members
    summary = lax.all_to_all(summary, NEAR, 0, 0, tiled=True)
    early = max(1, parts // 2)

    def reading(step):
        return reading_stage(first, step, parts, projected, halo, *entries[step], kept)

    reads = [reading(step) for step in range(early)]
    summary, reads = lax.optimization_barrier((summary, reads))
    *prefix, total = chain_stage(summary.reshape(members, own, DK, 2 * DK))
    starts = entry_stage(*prefix, entering_state(total))
    starts = lax.all_to_all(starts.reshape(heads, DK, DK), NEAR, 0, 0, tiled=True)
    reads += [reading(step) for step in range(early, parts)]
    return finish_stage(first, reads, starts, norm_gain)


def solution(mesh):
    seq, head = mesh.shape["seq"], mesh.shape["head"]
    inner = max(1, 16 // head)
    while seq % inner:
        inner //= 2
    layered = Mesh(mesh.devices.reshape(seq // inner, inner, head), ALL)
    in_specs = (
        P(ALL, None),
        P(None, "head"),
        P("head", ("outer", "inner")),
        P("head", ("outer", "inner")),
        P(),
    )
    return jax.shard_map(
        per_device, mesh=layered, in_specs=in_specs, out_specs=P(ALL, None), check_vma=False
    )
```

```python
import functools

import jax
import jax.numpy as jnp
from jax import lax
from jax.experimental import pallas as pl
from jax.experimental.pallas import tpu as pltpu
from jax.sharding import Mesh
from jax.sharding import PartitionSpec as P

DK = 128
V_GROUP = 2
KW = 4
STRETCH = 128
HALO = 8
BASE = 16
SEGMENTS = 2 + V_GROUP
GROUP_CHANNELS = (2 + V_GROUP) * DK
ALL = ("outer", "inner", "head")
NEAR = ("inner", "head")

f32 = jnp.float32
bf16 = jnp.bfloat16


LOG2E = 1.4426950408889634
VMEM = pl.BlockSpec(memory_space=pltpu.VMEM)
SMEM = pl.BlockSpec(memory_space=pltpu.SMEM)
FAR = pl.BlockSpec(memory_space=pltpu.HBM)


def near(array):
    return pltpu.with_memory_space_constraint(array, pltpu.VMEM)


def far(array):
    return pltpu.with_memory_space_constraint(array, pltpu.HBM)


def product(left, right):
    return jnp.dot(left, right, preferred_element_type=f32)


def part_at(first, step, parts):
    return lax.rem(first + step, parts)


def lanes_of(start):
    return pl.ds(pl.multiple_of(start, DK), DK)


def convolved(ext, cols, taps, c):
    start = c * STRETCH + HALO - (KW - 1)
    total = ext[start : start + STRETCH, cols] * taps[0:1]
    for j in range(1, KW):
        total = total + ext[start + j : start + j + STRETCH, cols] * taps[j : j + 1]
    half = 0.5 * total
    return (half + half * jnp.tanh(half)).astype(bf16)


def running_sum(gates):
    lane = lax.broadcasted_iota(jnp.int32, gates.shape, 1)
    total = gates
    for k in (1, 2, 4, 8, 16, 32, 64):
        total = total + jnp.where(lane >= k, pltpu.roll(total, k, 1), 0.0)
    return total


def square_iotas():
    row = lax.broadcasted_iota(jnp.int32, (STRETCH, STRETCH), 0)
    col = lax.broadcasted_iota(jnp.int32, (STRETCH, STRETCH), 1)
    return row, col


def block_inverses(lower):
    units = len(lower)
    blocks = STRETCH // BASE
    small_lane = lax.broadcasted_iota(jnp.int32, (BASE, STRETCH), 1)
    small_row = lax.broadcasted_iota(jnp.int32, (BASE, STRETCH), 0)
    owner = small_lane // BASE
    packed = []
    for unit in range(units):
        piece = lower[unit][0:BASE]
        for b in range(1, blocks):
            piece = jnp.where(owner == b, lower[unit][b * BASE : (b + 1) * BASE], piece)
        packed.append(piece)
    half = BASE // 2
    upper = jnp.concatenate([piece[:half] for piece in packed], axis=0)
    under = jnp.concatenate([piece[half:] for piece in packed], axis=0)
    group_start = (lax.broadcasted_iota(jnp.int32, upper.shape, 1) // BASE) * BASE
    start = jnp.where(small_lane % BASE == small_row, 1.0, 0.0).astype(f32)
    shape = (units, half, STRETCH)
    top = jnp.broadcast_to(start[None, :half], shape)
    bottom = jnp.broadcast_to(start[None, half:], shape)
    for j in range(BASE - 1):
        pivot = top[:, j : j + 1, :] if j < half else bottom[:, j - half : j - half + 1, :]
        if j < half - 1:
            top = top - jnp.take_along_axis(upper, group_start + j, axis=1).reshape(shape) * pivot
        bottom = bottom - jnp.take_along_axis(under, group_start + j, axis=1).reshape(shape) * pivot
    solved = [jnp.concatenate([top[unit], bottom[unit]], axis=0) for unit in range(units)]

    rows = [
        [jnp.where(owner == b, solved[unit], 0.0) for b in range(blocks)] for unit in range(units)
    ]
    size = BASE
    while size < STRETCH:
        per = size // BASE
        odd = [b for b in range(blocks) if (b // per) % 2 == 1]
        firsts = []
        for unit in range(units):
            crossing = [
                jnp.where(
                    small_lane // size == (b // per) - 1,
                    lower[unit][b * BASE : (b + 1) * BASE],
                    0.0,
                )
                for b in odd
            ]
            firsts.append(
                product(
                    jnp.concatenate(crossing, axis=0).astype(bf16),
                    jnp.concatenate(rows[unit], axis=0).astype(bf16),
                ).astype(bf16)
            )
        for unit in range(units):
            laid = [jnp.zeros((BASE, STRETCH), bf16)] * blocks
            for i, b in enumerate(odd):
                laid[b] = firsts[unit][i * BASE : (i + 1) * BASE]
            odd_rows = jnp.concatenate([rows[unit][b] for b in odd], axis=0)
            updated = odd_rows - product(odd_rows.astype(bf16), jnp.concatenate(laid, axis=0))
            for i, b in enumerate(odd):
                rows[unit][b] = updated[i * BASE : (i + 1) * BASE]
        size *= 2
    return [jnp.concatenate(rows[unit], axis=0) for unit in range(units)]


def pack_kernel(parts, first_ref, x_ref, gate_ref, rate_ref, taps_ref, halo_ref, *pack_refs):
    heads = gate_ref.shape[0]
    length = gate_ref.shape[1] // parts
    number = length // STRETCH
    segments = taps_ref.shape[1] // DK
    halo_ref[...] = x_ref[...]
    base = 2 * number * heads
    slots = [(ref, i) for ref in pack_refs for i in range(ref.shape[0])]
    for step, (ref, i) in enumerate(slots):
        first = part_at(first_ref[0], step, parts) * length
        for c in range(number):
            lanes = lanes_of(first + c * STRETCH)
            ref[i, c * heads : (c + 1) * heads] = gate_ref[:, lanes]
            ref[i, (number + c) * heads : (number + c + 1) * heads] = rate_ref[:, lanes]
        for segment in range(segments):
            rows = slice(base + segment * KW, base + (segment + 1) * KW)
            ref[i, rows] = taps_ref[:, segment * DK : (segment + 1) * DK].astype(f32)


def pack_stage(first, stacks, parts, projected, log_gate, write_rate, conv_weight):
    length, channels = projected.shape
    heads = log_gate.shape[0]
    rows = 2 * (length // STRETCH) * heads + conv_weight.shape[1] // DK * KW
    whole = lambda array: pl.BlockSpec(array.shape, lambda i: (0, 0))
    return pl.pallas_call(
        functools.partial(pack_kernel, parts),
        grid=(1,),
        in_specs=[
            SMEM,
            pl.BlockSpec((HALO, channels), lambda i: (length // HALO - 1, 0)),
            whole(log_gate),
            whole(write_rate),
            whole(conv_weight),
        ],
        out_specs=[VMEM] * (1 + len(stacks)),
        out_shape=[pltpu.VMEM((HALO, channels), bf16)]
        + [pltpu.VMEM((count, rows, DK), f32) for count in stacks],
        compiler_params=pltpu.CompilerParams(vmem_limit_bytes=2 << 20),
        name="pack_stage",
    )(first, far(projected), far(log_gate), far(write_rate), far(conv_weight))


def local_body(number, part, halo_ref, pack, block, ext, kept, norm_ref, arrived, ready):
    key_ref, summary_ref, written_ref, joint_ref = kept
    key_heads = norm_ref.shape[1]
    width = key_heads * GROUP_CHANNELS
    heads = key_heads * V_GROUP
    units = heads * number
    row, col = square_iotas()
    below = row > col
    eye = jnp.where(row == col, 1.0, 0.0).astype(f32)

    rates = pack[units : 2 * units]
    cumulative = running_sum(pack[0:units])
    grown = jnp.exp(cumulative)
    tail = jnp.exp(cumulative[:, STRETCH - 1 : STRETCH] - cumulative)
    bits = cumulative * LOG2E
    columns = jnp.transpose(bits + jnp.log2(rates), (1, 0))
    where = [(c, g) for g in range(key_heads) for c in range(number)]

    def units_of(c, g):
        return [(j, c * heads + g * V_GROUP + j) for j in range(V_GROUP)]

    def channels(c, g, kind):
        segment = g * SEGMENTS + kind
        cols = slice(segment * DK, (segment + 1) * DK)
        if c == 0:
            ext[0:HALO, cols] = halo_ref[:, lanes_of(part * width + segment * DK)].astype(f32)
            ext[HALO:, cols] = block[:, cols].astype(f32)
        at = 2 * units + segment * KW
        return convolved(ext, cols, pack[at : at + KW], c)

    keys, inverses, lower = {}, {}, [None] * units
    for c, g in where:
        if c == 0:
            arrived(g)
        k = channels(c, g, 1)
        keys[c, g] = k
        key_ref[c * STRETCH : (c + 1) * STRETCH, g * DK : (g + 1) * DK] = k
        gram = lax.dot_general(k, k, (((1,), (1,)), ((), ())), preferred_element_type=f32)
        diagonal = gram * eye
        sum_row = jnp.sum(diagonal, axis=0, keepdims=True) + 1e-06
        sum_col = jnp.sum(diagonal, axis=1, keepdims=True) + 1e-06
        inverses[c, g] = lax.rsqrt(sum_row)
        log_row, log_col = -0.5 * jnp.log2(sum_row), -0.5 * jnp.log2(sum_col)
        norm_ref[0, g, c : c + 1] = log_row
        for j, unit in units_of(c, g):
            spread = (columns[:, unit : unit + 1] + log_col) - (bits[unit : unit + 1] - log_row)
            lower[unit] = gram * jnp.exp2(jnp.where(below, spread, -1e30))

    ready(0)
    solved = block_inverses(lower)

    fresh, carried, scaled = [None] * units, [None] * units, [None] * units
    for c, g in where:
        turned = jnp.transpose(keys[c, g].astype(f32), (1, 0)) * inverses[c, g]
        for j, unit in units_of(c, g):
            at = slice(unit, unit + 1)
            by_rate = solved[unit] * rates[at]
            fresh[unit] = product(by_rate.astype(bf16), channels(c, g, 2 + j))
            by_rate = by_rate * (grown[at] * inverses[c, g])
            carried[unit] = product(by_rate.astype(bf16), keys[c, g])
            scaled[unit] = (turned * tail[at]).astype(bf16)

    nothing = jnp.zeros((STRETCH, DK), f32)
    joint = [jnp.concatenate([jnp.zeros((DK, DK), f32), eye], axis=1)] * heads
    for c in range(number):
        for head in range(heads):
            unit = c * heads + head
            if c == 0:
                written = jnp.concatenate([fresh[unit], -carried[unit]], axis=1)
            else:
                start = joint[head].astype(bf16)
                joint_ref[c - 1, head] = start
                written = jnp.concatenate([fresh[unit], nothing], axis=1) - product(
                    carried[unit].astype(bf16), start
                )
            written = written.astype(bf16)
            written_ref[c, head] = written
            decay = grown[unit : unit + 1, STRETCH - 1 : STRETCH]
            joint[head] = joint[head] * decay + product(scaled[unit], written)
        ready(2 + c)
        if c > 0:
            ready(1 + number + c)
    for head in range(heads):
        summary_ref[head, :, :DK] = joint[head][:, :DK].astype(bf16)
        summary_ref[head, :, DK:] = (joint[head][:, DK:] - eye).astype(bf16)
    ready(1)


def channel_copies(base, key_heads, x_ref, block, sems):
    used = (SEGMENTS - 1) * DK
    copies = []
    for g in range(key_heads):
        source = pl.ds(pl.multiple_of(base + (g * SEGMENTS + 1) * DK, DK), used)
        target = pl.ds((g * SEGMENTS + 1) * DK, used)
        copies.append(
            pltpu.make_async_copy(x_ref.at[:, source], block.at[:, target], sems.at[g])
        )
    return copies


def kept_copies(number, step, place, kept, outs, sems):
    key_ref, summary_ref, written_ref, joint_ref = kept
    pairs = [(key_ref, outs[3].at[step]), (summary_ref, outs[0].at[place])]
    pairs += [(written_ref.at[c], outs[1].at[step, c]) for c in range(number)]
    pairs += [(joint_ref.at[c - 1], outs[2].at[step, c]) for c in range(1, number)]
    return [
        pltpu.make_async_copy(source, target, sems.at[i]) for i, (source, target) in enumerate(pairs)
    ]


def first_kernel(number, parts, first_ref, x_ref, halo_ref, pack_ref, *refs):
    kept, (norm_ref, other, block, ext, sems, other_sems) = refs[:4], refs[4:]
    key_heads = norm_ref.shape[1]
    width = key_heads * GROUP_CHANNELS
    part, next_part = part_at(first_ref[0], 0, parts), part_at(first_ref[0], 1, parts)
    coming = channel_copies(part * width, key_heads, x_ref, block, sems)
    others = channel_copies(next_part * width, key_heads, x_ref, other, other_sems)
    for copy in coming + others:
        copy.start()
    local_body(
        number,
        part,
        halo_ref,
        pack_ref.at[0],
        block,
        ext,
        kept,
        norm_ref,
        lambda g: coming[g].wait(),
        lambda i: None,
    )
    for copy in others:
        copy.wait()


def second_kernel(number, parts, first_ref, halo_ref, pack_ref, block, *refs):
    before, outs, norm_ref, (ext, *kept, before_sems, sems) = refs[:4], refs[4:8], refs[8], refs[9:]
    heads = norm_ref.shape[1] * V_GROUP
    old, part = part_at(first_ref[0], 0, parts), part_at(first_ref[0], 1, parts)
    leaving = kept_copies(number, 0, pl.ds(old * heads, heads), before, outs, before_sems)
    for copy in leaving:
        copy.start()
    going = kept_copies(number, 1, pl.ds(part * heads, heads), kept, outs, sems)
    local_body(
        number,
        part,
        halo_ref,
        pack_ref.at[0],
        block,
        ext,
        kept,
        norm_ref,
        lambda g: None,
        lambda i: going[i].start(),
    )
    for copy in leaving + going:
        copy.wait()


def local_kernel(number, parts, stacks, first_ref, x_ref, halo_ref, *refs):
    pack_refs, refs = refs[: len(stacks)], refs[len(stacks) :]
    outs, norm_ref = refs[:4], refs[4]
    pack, blocks, ext, *held, in_sems, out_sems = refs[5:]
    step = pl.program_id(0)
    key_heads = norm_ref.shape[1]
    width = key_heads * GROUP_CHANNELS
    heads = key_heads * V_GROUP

    def arriving(at):
        here = lax.rem(at, 2)
        base = part_at(first_ref[0], at, parts) * width
        return channel_copies(base, key_heads, x_ref, blocks.at[here], in_sems.at[here])

    def leaving(at):
        here = lax.rem(at, 2)
        place = pl.ds(part_at(first_ref[0], at, parts) * heads, heads)
        kept = [ref.at[here] for ref in held]
        return kept_copies(number, at, place, kept, outs, out_sems.at[here])

    @pl.when(step == 0)
    def _():
        for copy in arriving(step):
            copy.start()

    @pl.when(step + 1 < pl.num_programs(0))
    def _():
        for copy in arriving(step + 1):
            copy.start()

    coming, going = arriving(step), leaving(step)
    entries = [(ref, i) for ref in pack_refs for i in range(ref.shape[0])]
    for n, (ref, i) in enumerate(entries):

        @pl.when(step == n)
        def _():
            pack[...] = ref[i]

    slot = lax.rem(step, 2)
    local_body(
        number,
        part_at(first_ref[0], step, parts),
        halo_ref,
        pack,
        blocks.at[slot],
        ext,
        [ref.at[slot] for ref in held],
        norm_ref,
        lambda g: coming[g].wait(),
        lambda i: going[i].start(),
    )

    @pl.when(step > 0)
    def _():
        for copy in leaving(step - 1):
            copy.wait()

    @pl.when(step + 1 == pl.num_programs(0))
    def _():
        for copy in going:
            copy.wait()


def kept_scratch(number, heads, length):
    return [
        ((length, heads // V_GROUP * DK), bf16),
        ((heads, DK, 2 * DK), bf16),
        ((number, heads, STRETCH, 2 * DK), bf16),
        ((max(1, number - 1), heads, STRETCH, 2 * DK), bf16),
    ]


def kept_arrays(parts, number, heads, length):
    per_unit = (parts, number, heads, STRETCH, 2 * DK)
    return [
        pltpu.HBM((heads * parts, DK, 2 * DK), bf16),
        pltpu.HBM(per_unit, bf16),
        pltpu.HBM(per_unit, bf16),
        pltpu.HBM((parts, length, heads // V_GROUP * DK), bf16),
    ]


def local_stage(first, parts, projected, halo, packs):
    length, channels = projected.shape
    number = length // STRETCH
    width = channels // parts
    key_heads = width // GROUP_CHANNELS
    heads = key_heads * V_GROUP
    scratch = kept_scratch(number, heads, length)
    kept = kept_arrays(parts, number, heads, length)
    norms = (1, key_heads, number, STRETCH)
    ext = pltpu.VMEM((HALO + length, width), f32)
    results = 2 * number + 1
    if len(packs) == 2:
        *before, norm, block = pl.pallas_call(
            functools.partial(first_kernel, number, parts),
            in_specs=[SMEM, FAR, VMEM, VMEM],
            out_specs=[VMEM] * 6,
            out_shape=[pltpu.VMEM(*shape) for shape in scratch]
            + [pltpu.VMEM(norms, f32), pltpu.VMEM((length, width), bf16)],
            scratch_shapes=[
                pltpu.VMEM((length, width), bf16),
                ext,
                pltpu.SemaphoreType.DMA((key_heads,)),
                pltpu.SemaphoreType.DMA((key_heads,)),
            ],
            compiler_params=pltpu.CompilerParams(vmem_limit_bytes=24 << 20),
            name="first_stage",
        )(first, far(projected), near(halo), near(packs[0]))
        *made, other_norm = pl.pallas_call(
            functools.partial(second_kernel, number, parts),
            in_specs=[SMEM] + [VMEM] * 7,
            out_specs=[FAR] * 4 + [VMEM],
            out_shape=kept + [pltpu.VMEM(norms, f32)],
            scratch_shapes=[ext]
            + [pltpu.VMEM(*shape) for shape in scratch]
            + [pltpu.SemaphoreType.DMA((results,))] * 2,
            compiler_params=pltpu.CompilerParams(vmem_limit_bytes=24 << 20),
            name="second_stage",
        )(first, near(halo), near(packs[1]), block, *before)
        return *made, [(norm, 0), (other_norm, 0)]
    *made, norm = pl.pallas_call(
        functools.partial(local_kernel, number, parts, tuple(p.shape[0] for p in packs)),
        grid=(parts,),
        in_specs=[SMEM, FAR] + [VMEM] * (1 + len(packs)),
        out_specs=[FAR] * 4 + [pl.BlockSpec(norms, lambda p: (p, 0, 0, 0))],
        out_shape=kept + [jax.ShapeDtypeStruct((parts,) + norms[1:], f32)],
        scratch_shapes=[
            pltpu.VMEM(packs[0].shape[1:], f32),
            pltpu.VMEM((2, length, width), bf16),
            ext,
            *(pltpu.VMEM((2,) + shape, dtype) for shape, dtype in scratch),
            pltpu.SemaphoreType.DMA((2, key_heads)),
            pltpu.SemaphoreType.DMA((2, results)),
        ],
        compiler_params=pltpu.CompilerParams(vmem_limit_bytes=44 << 20),
        name="local_stage",
    )(first, far(projected), near(halo), *(near(p) for p in packs))
    return *made, [(norm, p) for p in range(parts)]


def reading_kernel(number, index, first_ref, x_ref, halo_ref, pack_ref, *refs):
    written_ref, joint_ref, key_ref, norm_ref, out_ref, reach_ref, ext = refs
    heads = pl.num_programs(0) * V_GROUP
    g = pl.program_id(0)
    units = heads * number
    row, col = square_iotas()
    inside = row >= col
    gates = [
        pack_ref[index, pl.ds(c * heads + g * V_GROUP, V_GROUP)] for c in range(number)
    ]
    cumulative = running_sum(jnp.concatenate(gates, axis=0))
    bits = cumulative * LOG2E
    columns = jnp.transpose(bits, (1, 0))
    ext[0:HALO] = halo_ref[...].astype(f32)
    ext[HALO:] = x_ref[...].astype(f32)
    taps = pack_ref[index, pl.ds(2 * units + g * SEGMENTS * KW, KW)]
    for c in range(number):
        rows = slice(c * STRETCH, (c + 1) * STRETCH)
        query = convolved(ext, slice(0, DK), taps, c)
        gram = lax.dot_general(
            query, key_ref[0, rows], (((1,), (1,)), ((), ())), preferred_element_type=f32
        )
        log_row = norm_ref[0, pl.ds(g, 1), c]
        for j in range(V_GROUP):
            unit = c * V_GROUP + j
            sum_here = columns[:, unit : unit + 1]
            spread = sum_here - (bits[unit : unit + 1] - log_row)
            decay = jnp.exp2(jnp.where(inside, spread, -1e30))
            result = product((gram * decay).astype(bf16), written_ref[0, c, j])
            grown = jnp.exp2(sum_here)
            if c == 0:
                reached = result[:, DK:] + grown * query.astype(f32)
            else:
                result = result + grown * product(query, joint_ref[0, c, j])
                reached = result[:, DK:]
            out_ref[j, rows] = result[:, :DK].astype(bf16)
            reach_ref[j, rows] = reached.astype(bf16)


def reading_stage(first, step, parts, projected, halo, packs, index, kept):
    length, channels = projected.shape
    number = length // STRETCH
    key_heads = channels // parts // GROUP_CHANNELS
    heads = key_heads * V_GROUP
    written, joints, keys, norms = kept
    norm, norm_at = norms[step]
    query = lambda g, first: (0, (part_at(first[0], step, parts) * key_heads + g) * SEGMENTS)
    per_unit = pl.BlockSpec(
        (1, number, V_GROUP, STRETCH, 2 * DK), lambda g, first: (step, 0, g, 0, 0)
    )
    per_head = pl.BlockSpec((V_GROUP, length, DK), lambda g, first: (g, 0, 0))
    return pl.pallas_call(
        functools.partial(reading_kernel, number, index),
        grid_spec=pltpu.PrefetchScalarGridSpec(
            num_scalar_prefetch=1,
            grid=(key_heads,),
            in_specs=[
                pl.BlockSpec((length, DK), query),
                pl.BlockSpec((HALO, DK), query),
                pl.BlockSpec(packs.shape, lambda g, first: (0, 0, 0)),
                per_unit,
                per_unit,
                pl.BlockSpec((1, length, DK), lambda g, first: (step, 0, g)),
                pl.BlockSpec((1,) + norm.shape[1:], lambda g, first: (norm_at, 0, 0, 0)),
            ],
            out_specs=[per_head, per_head],
            scratch_shapes=[pltpu.VMEM((HALO + length, DK), f32)],
        ),
        out_shape=[pltpu.HBM((heads, length, DK), bf16)] * 2,
        compiler_params=pltpu.CompilerParams(vmem_limit_bytes=12 << 20),
        name="reading_stage",
    )(first, far(projected), halo, packs, far(written), far(joints), far(keys), norm)


def advance(joint, loss, gain):
    high = joint.astype(bf16)
    low = (joint - high.astype(f32)).astype(bf16)
    return joint + (product(loss, high) + product(loss, low)) + gain


def chain_kernel(run, summary_ref, state_ref, loss_ref, sub_ref, total_ref):
    devices, heads = summary_ref.shape[0], summary_ref.shape[1]
    row, col = square_iotas()
    eye = jnp.where(row == col, 1.0, 0.0).astype(f32)
    nothing = jnp.zeros((DK, DK), f32)
    start = jnp.concatenate([nothing, eye], axis=1)
    for h in range(heads):
        joint = [start] * (devices // run)
        for k in range(run):
            for i in range(devices // run):
                d = i * run + k
                state_ref[d, h] = joint[i][:, :DK]
                loss_ref[d, h] = (joint[i][:, DK:] - eye).astype(bf16)
                gain = jnp.concatenate([summary_ref[d, h, :, :DK].astype(f32), nothing], axis=1)
                joint[i] = advance(joint[i], summary_ref[d, h, :, DK:], gain)
        total = joint[0]
        for i in range(devices // run):
            sub_ref[i, h] = joint[i]
            if i > 0:
                gain = jnp.concatenate([joint[i][:, :DK], nothing], axis=1)
                total = advance(total, (joint[i][:, DK:] - eye).astype(bf16), gain)
        total_ref[h] = total


def chain_stage(summary):
    devices, heads = summary.shape[:2]
    run = 4 if devices % 4 == 0 else devices
    return pl.pallas_call(
        functools.partial(chain_kernel, run),
        in_specs=[VMEM],
        out_specs=[VMEM] * 4,
        out_shape=[
            pltpu.VMEM((devices, heads, DK, DK), f32),
            pltpu.VMEM((devices, heads, DK, DK), bf16),
            pltpu.VMEM((devices // run, heads, DK, 2 * DK), f32),
            pltpu.VMEM((heads, DK, 2 * DK), f32),
        ],
        compiler_params=pltpu.CompilerParams(vmem_limit_bytes=12 << 20),
        name="chain_stage",
    )(near(summary))


def entry_kernel(state_ref, loss_ref, sub_ref, entering_ref, start_ref):
    devices, heads = state_ref.shape[0], state_ref.shape[1]
    runs = sub_ref.shape[0]
    run = devices // runs
    row, col = square_iotas()
    eye = jnp.where(row == col, 1.0, 0.0).astype(f32)
    for h in range(heads):
        entering = [entering_ref[h]]
        for i in range(runs - 1):
            loss = (sub_ref[i, h, :, DK:] - eye).astype(bf16)
            entering.append(advance(entering[i], loss, sub_ref[i, h, :, :DK]))
        for d in range(devices):
            start = advance(entering[d // run], loss_ref[d, h], state_ref[d, h])
            start_ref[d, h] = start.astype(bf16)


def entry_stage(states, losses, subs, entering):
    devices, heads = states.shape[:2]
    return pl.pallas_call(
        entry_kernel,
        in_specs=[VMEM] * 4,
        out_specs=VMEM,
        out_shape=jax.ShapeDtypeStruct((devices, heads, DK, DK), bf16),
        compiler_params=pltpu.CompilerParams(vmem_limit_bytes=12 << 20),
        name="entry_stage",
    )(states, losses, subs, near(entering))


def finish_kernel(batch, first_ref, start_ref, gain_ref, *refs):
    reads, refs = refs[:-7], refs[-7:]
    out_ref, gain, held_local, held_reach, done, in_sems, out_sems = refs
    parts = len(reads) // 2
    heads = reads[0].shape[0]
    arriving, leaving = [], []
    gain_copy = pltpu.make_async_copy(gain_ref, gain, in_sems.at[0, out_sems.shape[0]])
    gain_copy.start()
    for p in range(parts):
        for b in range(heads // batch):
            at = pl.ds(b * batch, batch)
            into = pl.ds(p * heads + b * batch, batch)
            n = len(arriving)
            arriving.append(
                (
                    pltpu.make_async_copy(
                        reads[2 * p].at[at], held_local.at[into], in_sems.at[0, n]
                    ),
                    pltpu.make_async_copy(
                        reads[2 * p + 1].at[at], held_reach.at[into], in_sems.at[1, n]
                    ),
                )
            )
            for copy in arriving[-1]:
                copy.start()
    gain_copy.wait()
    for p in range(parts):
        part = part_at(first_ref[0], p, parts)
        for b in range(heads // batch):
            n = len(leaving)
            for copy in arriving[n]:
                copy.wait()
            for k in range(batch):
                h = p * heads + b * batch + k
                start = start_ref[part * heads + b * batch + k]
                result = held_local[h].astype(f32) + product(held_reach[h], start)
                mean = jnp.mean(result * result, axis=1, keepdims=True)
                scaled = result * lax.rsqrt(mean + 1e-06) * gain[...]
                done[:, h * DK : (h + 1) * DK] = scaled.astype(bf16)
            width = batch * DK
            to = pl.ds(pl.multiple_of((part * heads + b * batch) * DK, DK), width)
            leaving.append(
                pltpu.make_async_copy(
                    done.at[:, pl.ds(n * width, width)], out_ref.at[:, to], out_sems.at[n]
                )
            )
            leaving[-1].start()
    for copy in leaving:
        copy.wait()


def finish_stage(first, reads, starts, gain):
    heads, length, _ = reads[0][0].shape
    all_heads = starts.shape[0]
    batch = 2
    return pl.pallas_call(
        functools.partial(finish_kernel, batch),
        in_specs=[SMEM, VMEM, FAR] + [FAR] * (2 * len(reads)),
        out_specs=FAR,
        out_shape=pltpu.HBM((length, all_heads * DK), bf16),
        scratch_shapes=[
            pltpu.VMEM((1, DK), f32),
            pltpu.VMEM((all_heads, length, DK), bf16),
            pltpu.VMEM((all_heads, length, DK), bf16),
            pltpu.VMEM((length, all_heads * DK), bf16),
            pltpu.SemaphoreType.DMA((2, all_heads // batch + 1)),
            pltpu.SemaphoreType.DMA((all_heads // batch,)),
        ],
        compiler_params=pltpu.CompilerParams(vmem_limit_bytes=16 << 20),
        name="finish_stage",
    )(first, near(starts), far(gain.reshape(1, DK)), *(far(a) for read in reads for a in read))


def entering_state(total):
    outer = lax.axis_size("outer")
    if outer == 1:
        return jnp.zeros_like(total[..., :DK])
    if outer == 2:
        return lax.ppermute(total[..., :DK], "outer", [(0, 1)])
    everyone = lax.all_gather(total, "outer", axis=0)
    mine = lax.axis_index("outer")

    def step(i, state):
        piece = lax.dynamic_index_in_dim(everyone, i, 0, keepdims=False)
        moved = piece[..., :DK] + jnp.einsum(
            "hij,hjk->hik", piece[..., DK:], state, precision=lax.Precision.HIGHEST
        )
        return jnp.where(i < mine, moved, state)

    return lax.fori_loop(0, outer - 1, step, jnp.zeros_like(total[..., :DK]))


def per_device(projected, conv_weight, log_gate, write_rate, norm_gain):
    devices = lax.axis_size(ALL)
    parts = lax.axis_size("head")
    route = [(i, i + 1) for i in range(devices - 1)]
    arguments = (projected, log_gate, write_rate, conv_weight)
    if parts == 2:
        first = lax.axis_index("head").astype(jnp.int32).reshape(1)
        tail, mine, theirs = pack_stage(first, (1, 1), parts, *arguments)
        halo = lax.ppermute(tail, ALL, route)
        packs = [mine, lax.ppermute(theirs, "head", [(0, 1), (1, 0)])]
    else:
        first = jnp.zeros((1,), jnp.int32)
        tail, mine = pack_stage(first, (parts,), parts, *arguments)
        halo = lax.ppermute(tail, ALL, route)
        packs = [lax.all_to_all(mine, "head", 0, 0, tiled=True)]
    entries = [(pack, i) for pack in packs for i in range(pack.shape[0])]

    summary, *kept = local_stage(first, parts, projected, halo, packs)
    heads = summary.shape[0]
    members = lax.axis_size(NEAR)
    own = heads // members
    summary = lax.all_to_all(summary, NEAR, 0, 0, tiled=True)
    early = max(1, parts // 2)

    def reading(step):
        return reading_stage(first, step, parts, projected, halo, *entries[step], kept)

    reads = [reading(step) for step in range(early)]
    summary, reads = lax.optimization_barrier((summary, reads))
    *prefix, total = chain_stage(summary.reshape(members, own, DK, 2 * DK))
    starts = entry_stage(*prefix, entering_state(total))
    starts = lax.all_to_all(starts.reshape(heads, DK, DK), NEAR, 0, 0, tiled=True)
    reads += [reading(step) for step in range(early, parts)]
    return finish_stage(first, reads, starts, norm_gain)


def solution(mesh):
    seq, head = mesh.shape["seq"], mesh.shape["head"]
    inner = max(1, 16 // head)
    while seq % inner:
        inner //= 2
    layered = Mesh(mesh.devices.reshape(seq // inner, inner, head), ALL)
    in_specs = (
        P(ALL, None),
        P(None, "head"),
        P("head", ("outer", "inner")),
        P("head", ("outer", "inner")),
        P(),
    )
    return jax.shard_map(
        per_device, mesh=layered, in_specs=in_specs, out_specs=P(ALL, None), check_vma=False
    )
```

```python
import functools

import jax
import jax.numpy as jnp
from jax import lax
from jax.experimental import pallas as pl
from jax.experimental.pallas import tpu as pltpu
from jax.sharding import Mesh
from jax.sharding import PartitionSpec as P

DK = 128
V_GROUP = 2
KW = 4
STRETCH = 128
HALO = 8
BASE = 16
SEGMENTS = 2 + V_GROUP
GROUP_CHANNELS = (2 + V_GROUP) * DK
ALL = ("outer", "inner", "head")
NEAR = ("inner", "head")

f32 = jnp.float32
bf16 = jnp.bfloat16


LOG2E = 1.4426950408889634
VMEM = pl.BlockSpec(memory_space=pltpu.VMEM)
SMEM = pl.BlockSpec(memory_space=pltpu.SMEM)
FAR = pl.BlockSpec(memory_space=pltpu.HBM)


def near(array):
    return pltpu.with_memory_space_constraint(array, pltpu.VMEM)


def far(array):
    return pltpu.with_memory_space_constraint(array, pltpu.HBM)


def product(left, right):
    return jnp.dot(left, right, preferred_element_type=f32)


def part_at(first, step, parts):
    return lax.rem(first + step, parts)


def lanes_of(start):
    return pl.ds(pl.multiple_of(start, DK), DK)


def halves(array):
    high = array.astype(bf16)
    return high, (array - high.astype(f32)).astype(bf16)


def product_left(left, right):
    high, low = halves(left)
    both = product(jnp.concatenate([high, low], axis=0), right)
    return both[: left.shape[0]] + both[left.shape[0] :]


def convolved(ext, cols, taps, c):
    start = c * STRETCH + HALO - (KW - 1)
    total = ext[start : start + STRETCH, cols] * taps[0:1]
    for j in range(1, KW):
        total = total + ext[start + j : start + j + STRETCH, cols] * taps[j : j + 1]
    half = 0.5 * total
    return (half + half * jnp.tanh(half)).astype(bf16)


def running_sum(gates):
    lane = lax.broadcasted_iota(jnp.int32, gates.shape, 1)
    total = gates
    for k in (1, 2, 4, 8, 16, 32, 64):
        total = total + jnp.where(lane >= k, pltpu.roll(total, k, 1), 0.0)
    return total


def square_iotas():
    row = lax.broadcasted_iota(jnp.int32, (STRETCH, STRETCH), 0)
    col = lax.broadcasted_iota(jnp.int32, (STRETCH, STRETCH), 1)
    return row, col


def block_inverses(lower):
    units = len(lower)
    blocks = STRETCH // BASE
    small_lane = lax.broadcasted_iota(jnp.int32, (BASE, STRETCH), 1)
    small_row = lax.broadcasted_iota(jnp.int32, (BASE, STRETCH), 0)
    owner = small_lane // BASE
    packed = []
    for unit in range(units):
        piece = lower[unit][0:BASE]
        for b in range(1, blocks):
            piece = jnp.where(owner == b, lower[unit][b * BASE : (b + 1) * BASE], piece)
        packed.append(piece)
    half = BASE // 2
    upper = jnp.concatenate([piece[:half] for piece in packed], axis=0)
    under = jnp.concatenate([piece[half:] for piece in packed], axis=0)
    group_start = (lax.broadcasted_iota(jnp.int32, upper.shape, 1) // BASE) * BASE
    start = jnp.where(small_lane % BASE == small_row, 1.0, 0.0).astype(f32)
    shape = (units, half, STRETCH)
    top = jnp.broadcast_to(start[None, :half], shape)
    bottom = jnp.broadcast_to(start[None, half:], shape)
    for j in range(BASE - 1):
        pivot = top[:, j : j + 1, :] if j < half else bottom[:, j - half : j - half + 1, :]
        if j < half - 1:
            top = top - jnp.take_along_axis(upper, group_start + j, axis=1).reshape(shape) * pivot
        bottom = bottom - jnp.take_along_axis(under, group_start + j, axis=1).reshape(shape) * pivot
    solved = [jnp.concatenate([top[unit], bottom[unit]], axis=0) for unit in range(units)]

    rows = [
        [jnp.where(owner == b, solved[unit], 0.0) for b in range(blocks)] for unit in range(units)
    ]
    size = BASE
    while size < STRETCH:
        per = size // BASE
        odd = [b for b in range(blocks) if (b // per) % 2 == 1]
        firsts = []
        for unit in range(units):
            crossing = [
                jnp.where(
                    small_lane // size == (b // per) - 1,
                    lower[unit][b * BASE : (b + 1) * BASE],
                    0.0,
                )
                for b in odd
            ]
            firsts.append(
                product(
                    jnp.concatenate(crossing, axis=0).astype(bf16),
                    jnp.concatenate(rows[unit], axis=0).astype(bf16),
                ).astype(bf16)
            )
        for unit in range(units):
            laid = [jnp.zeros((BASE, STRETCH), bf16)] * blocks
            for i, b in enumerate(odd):
                laid[b] = firsts[unit][i * BASE : (i + 1) * BASE]
            odd_rows = jnp.concatenate([rows[unit][b] for b in odd], axis=0)
            updated = odd_rows - product(odd_rows.astype(bf16), jnp.concatenate(laid, axis=0))
            for i, b in enumerate(odd):
                rows[unit][b] = updated[i * BASE : (i + 1) * BASE]
        size *= 2
    return [jnp.concatenate(rows[unit], axis=0) for unit in range(units)]


def pack_kernel(parts, first_ref, x_ref, gate_ref, rate_ref, taps_ref, halo_ref, *pack_refs):
    heads = gate_ref.shape[0]
    length = gate_ref.shape[1] // parts
    number = length // STRETCH
    segments = taps_ref.shape[1] // DK
    halo_ref[...] = x_ref[...]
    base = 2 * number * heads
    slots = [(ref, i) for ref in pack_refs for i in range(ref.shape[0])]
    for step, (ref, i) in enumerate(slots):
        first = part_at(first_ref[0], step, parts) * length
        for c in range(number):
            lanes = lanes_of(first + c * STRETCH)
            ref[i, c * heads : (c + 1) * heads] = gate_ref[:, lanes]
            ref[i, (number + c) * heads : (number + c + 1) * heads] = rate_ref[:, lanes]
        for segment in range(segments):
            rows = slice(base + segment * KW, base + (segment + 1) * KW)
            ref[i, rows] = taps_ref[:, segment * DK : (segment + 1) * DK].astype(f32)


def pack_stage(first, stacks, parts, projected, log_gate, write_rate, conv_weight):
    length, channels = projected.shape
    heads = log_gate.shape[0]
    rows = 2 * (length // STRETCH) * heads + conv_weight.shape[1] // DK * KW
    whole = lambda array: pl.BlockSpec(array.shape, lambda i: (0, 0))
    return pl.pallas_call(
        functools.partial(pack_kernel, parts),
        grid=(1,),
        in_specs=[
            SMEM,
            pl.BlockSpec((HALO, channels), lambda i: (length // HALO - 1, 0)),
            whole(log_gate),
            whole(write_rate),
            whole(conv_weight),
        ],
        out_specs=[VMEM] * (1 + len(stacks)),
        out_shape=[pltpu.VMEM((HALO, channels), bf16)]
        + [pltpu.VMEM((count, rows, DK), f32) for count in stacks],
        compiler_params=pltpu.CompilerParams(vmem_limit_bytes=2 << 20),
        name="pack_stage",
    )(first, far(projected), far(log_gate), far(write_rate), far(conv_weight))


def local_body(number, part, halo_ref, pack, block, ext, kept, norm_ref, arrived, ready):
    key_ref, summary_ref, written_ref, joint_ref = kept
    key_heads = norm_ref.shape[1]
    width = key_heads * GROUP_CHANNELS
    heads = key_heads * V_GROUP
    units = heads * number
    row, col = square_iotas()
    below = row > col
    eye = jnp.where(row == col, 1.0, 0.0).astype(f32)

    rates = pack[units : 2 * units]
    cumulative = running_sum(pack[0:units])
    grown = jnp.exp(cumulative)
    tail = jnp.exp(cumulative[:, STRETCH - 1 : STRETCH] - cumulative)
    bits = cumulative * LOG2E
    columns = jnp.transpose(bits + jnp.log2(rates), (1, 0))
    where = [(c, g) for g in range(key_heads) for c in range(number)]

    def units_of(c, g):
        return [(j, c * heads + g * V_GROUP + j) for j in range(V_GROUP)]

    def channels(c, g, kind):
        segment = g * SEGMENTS + kind
        cols = slice(segment * DK, (segment + 1) * DK)
        if c == 0:
            ext[0:HALO, cols] = halo_ref[:, lanes_of(part * width + segment * DK)].astype(f32)
            ext[HALO:, cols] = block[:, cols].astype(f32)
        at = 2 * units + segment * KW
        return convolved(ext, cols, pack[at : at + KW], c)

    keys, inverses, lower = {}, {}, [None] * units
    for c, g in where:
        if c == 0:
            arrived(g)
        k = channels(c, g, 1)
        keys[c, g] = k
        key_ref[c * STRETCH : (c + 1) * STRETCH, g * DK : (g + 1) * DK] = k
        gram = lax.dot_general(k, k, (((1,), (1,)), ((), ())), preferred_element_type=f32)
        diagonal = gram * eye
        sum_row = jnp.sum(diagonal, axis=0, keepdims=True) + 1e-06
        sum_col = jnp.sum(diagonal, axis=1, keepdims=True) + 1e-06
        inverses[c, g] = lax.rsqrt(sum_row)
        log_row, log_col = -0.5 * jnp.log2(sum_row), -0.5 * jnp.log2(sum_col)
        norm_ref[0, g, c : c + 1] = log_row
        for j, unit in units_of(c, g):
            spread = (columns[:, unit : unit + 1] + log_col) - (bits[unit : unit + 1] - log_row)
            lower[unit] = gram * jnp.exp2(jnp.where(below, spread, -1e30))

    ready(0)
    solved = block_inverses(lower)

    fresh, carried, scaled = [None] * units, [None] * units, [None] * units
    for c, g in where:
        turned = jnp.transpose(keys[c, g].astype(f32), (1, 0)) * inverses[c, g]
        for j, unit in units_of(c, g):
            at = slice(unit, unit + 1)
            by_rate = solved[unit] * rates[at]
            fresh[unit] = product_left(by_rate, channels(c, g, 2 + j))
            by_rate = by_rate * (grown[at] * inverses[c, g])
            carried[unit] = product_left(by_rate, keys[c, g])
            scaled[unit] = (turned * tail[at]).astype(bf16)

    nothing = jnp.zeros((STRETCH, DK), f32)
    joint = [jnp.concatenate([jnp.zeros((DK, DK), f32), eye], axis=1)] * heads
    for c in range(number):
        for head in range(heads):
            unit = c * heads + head
            if c == 0:
                written = jnp.concatenate([fresh[unit], -carried[unit]], axis=1)
            else:
                start = joint[head].astype(bf16)
                joint_ref[c - 1, head] = start
                written = jnp.concatenate([fresh[unit], nothing], axis=1) - product(
                    carried[unit].astype(bf16), start
                )
            written = written.astype(bf16)
            written_ref[c, head] = written
            decay = grown[unit : unit + 1, STRETCH - 1 : STRETCH]
            joint[head] = joint[head] * decay + product(scaled[unit], written)
        ready(2 + c)
        if c > 0:
            ready(1 + number + c)
    for head in range(heads):
        summary_ref[head, :, :DK] = joint[head][:, :DK].astype(bf16)
        summary_ref[head, :, DK:] = (joint[head][:, DK:] - eye).astype(bf16)
    ready(1)


def channel_copies(base, key_heads, x_ref, block, sems):
    used = (SEGMENTS - 1) * DK
    copies = []
    for g in range(key_heads):
        source = pl.ds(pl.multiple_of(base + (g * SEGMENTS + 1) * DK, DK), used)
        target = pl.ds((g * SEGMENTS + 1) * DK, used)
        copies.append(
            pltpu.make_async_copy(x_ref.at[:, source], block.at[:, target], sems.at[g])
        )
    return copies


def kept_copies(number, step, place, kept, outs, sems):
    key_ref, summary_ref, written_ref, joint_ref = kept
    pairs = [(key_ref, outs[3].at[step]), (summary_ref, outs[0].at[place])]
    pairs += [(written_ref.at[c], outs[1].at[step, c]) for c in range(number)]
    pairs += [(joint_ref.at[c - 1], outs[2].at[step, c]) for c in range(1, number)]
    return [
        pltpu.make_async_copy(source, target, sems.at[i]) for i, (source, target) in enumerate(pairs)
    ]


def first_kernel(number, parts, first_ref, x_ref, halo_ref, pack_ref, *refs):
    kept, (norm_ref, other, block, ext, sems, other_sems) = refs[:4], refs[4:]
    key_heads = norm_ref.shape[1]
    width = key_heads * GROUP_CHANNELS
    part, next_part = part_at(first_ref[0], 0, parts), part_at(first_ref[0], 1, parts)
    coming = channel_copies(part * width, key_heads, x_ref, block, sems)
    others = channel_copies(next_part * width, key_heads, x_ref, other, other_sems)
    for copy in coming + others:
        copy.start()
    local_body(
        number,
        part,
        halo_ref,
        pack_ref.at[0],
        block,
        ext,
        kept,
        norm_ref,
        lambda g: coming[g].wait(),
        lambda i: None,
    )
    for copy in others:
        copy.wait()


def second_kernel(number, parts, first_ref, halo_ref, pack_ref, block, *refs):
    before, outs, norm_ref, (ext, *kept, before_sems, sems) = refs[:4], refs[4:8], refs[8], refs[9:]
    heads = norm_ref.shape[1] * V_GROUP
    old, part = part_at(first_ref[0], 0, parts), part_at(first_ref[0], 1, parts)
    leaving = kept_copies(number, 0, pl.ds(old * heads, heads), before, outs, before_sems)
    for copy in leaving:
        copy.start()
    going = kept_copies(number, 1, pl.ds(part * heads, heads), kept, outs, sems)
    local_body(
        number,
        part,
        halo_ref,
        pack_ref.at[0],
        block,
        ext,
        kept,
        norm_ref,
        lambda g: None,
        lambda i: going[i].start(),
    )
    for copy in leaving + going:
        copy.wait()


def local_kernel(number, parts, stacks, first_ref, x_ref, halo_ref, *refs):
    pack_refs, refs = refs[: len(stacks)], refs[len(stacks) :]
    outs, norm_ref = refs[:4], refs[4]
    pack, blocks, ext, *held, in_sems, out_sems = refs[5:]
    step = pl.program_id(0)
    key_heads = norm_ref.shape[1]
    width = key_heads * GROUP_CHANNELS
    heads = key_heads * V_GROUP

    def arriving(at):
        here = lax.rem(at, 2)
        base = part_at(first_ref[0], at, parts) * width
        return channel_copies(base, key_heads, x_ref, blocks.at[here], in_sems.at[here])

    def leaving(at):
        here = lax.rem(at, 2)
        place = pl.ds(part_at(first_ref[0], at, parts) * heads, heads)
        kept = [ref.at[here] for ref in held]
        return kept_copies(number, at, place, kept, outs, out_sems.at[here])

    @pl.when(step == 0)
    def _():
        for copy in arriving(step):
            copy.start()

    @pl.when(step + 1 < pl.num_programs(0))
    def _():
        for copy in arriving(step + 1):
            copy.start()

    coming, going = arriving(step), leaving(step)
    entries = [(ref, i) for ref in pack_refs for i in range(ref.shape[0])]
    for n, (ref, i) in enumerate(entries):

        @pl.when(step == n)
        def _():
            pack[...] = ref[i]

    slot = lax.rem(step, 2)
    local_body(
        number,
        part_at(first_ref[0], step, parts),
        halo_ref,
        pack,
        blocks.at[slot],
        ext,
        [ref.at[slot] for ref in held],
        norm_ref,
        lambda g: coming[g].wait(),
        lambda i: going[i].start(),
    )

    @pl.when(step > 0)
    def _():
        for copy in leaving(step - 1):
            copy.wait()

    @pl.when(step + 1 == pl.num_programs(0))
    def _():
        for copy in going:
            copy.wait()


def kept_scratch(number, heads, length):
    return [
        ((length, heads // V_GROUP * DK), bf16),
        ((heads, DK, 2 * DK), bf16),
        ((number, heads, STRETCH, 2 * DK), bf16),
        ((max(1, number - 1), heads, STRETCH, 2 * DK), bf16),
    ]


def kept_arrays(parts, number, heads, length):
    per_unit = (parts, number, heads, STRETCH, 2 * DK)
    return [
        pltpu.HBM((heads * parts, DK, 2 * DK), bf16),
        pltpu.HBM(per_unit, bf16),
        pltpu.HBM(per_unit, bf16),
        pltpu.HBM((parts, length, heads // V_GROUP * DK), bf16),
    ]


def local_stage(first, parts, projected, halo, packs):
    length, channels = projected.shape
    number = length // STRETCH
    width = channels // parts
    key_heads = width // GROUP_CHANNELS
    heads = key_heads * V_GROUP
    scratch = kept_scratch(number, heads, length)
    kept = kept_arrays(parts, number, heads, length)
    norms = (1, key_heads, number, STRETCH)
    ext = pltpu.VMEM((HALO + length, width), f32)
    results = 2 * number + 1
    if len(packs) == 2:
        *before, norm, block = pl.pallas_call(
            functools.partial(first_kernel, number, parts),
            in_specs=[SMEM, FAR, VMEM, VMEM],
            out_specs=[VMEM] * 6,
            out_shape=[pltpu.VMEM(*shape) for shape in scratch]
            + [pltpu.VMEM(norms, f32), pltpu.VMEM((length, width), bf16)],
            scratch_shapes=[
                pltpu.VMEM((length, width), bf16),
                ext,
                pltpu.SemaphoreType.DMA((key_heads,)),
                pltpu.SemaphoreType.DMA((key_heads,)),
            ],
            compiler_params=pltpu.CompilerParams(vmem_limit_bytes=24 << 20),
            name="first_stage",
        )(first, far(projected), near(halo), near(packs[0]))
        *made, other_norm = pl.pallas_call(
            functools.partial(second_kernel, number, parts),
            in_specs=[SMEM] + [VMEM] * 7,
            out_specs=[FAR] * 4 + [VMEM],
            out_shape=kept + [pltpu.VMEM(norms, f32)],
            scratch_shapes=[ext]
            + [pltpu.VMEM(*shape) for shape in scratch]
            + [pltpu.SemaphoreType.DMA((results,))] * 2,
            compiler_params=pltpu.CompilerParams(vmem_limit_bytes=24 << 20),
            name="second_stage",
        )(first, near(halo), near(packs[1]), block, *before)
        return *made, [(norm, 0), (other_norm, 0)]
    *made, norm = pl.pallas_call(
        functools.partial(local_kernel, number, parts, tuple(p.shape[0] for p in packs)),
        grid=(parts,),
        in_specs=[SMEM, FAR] + [VMEM] * (1 + len(packs)),
        out_specs=[FAR] * 4 + [pl.BlockSpec(norms, lambda p: (p, 0, 0, 0))],
        out_shape=kept + [jax.ShapeDtypeStruct((parts,) + norms[1:], f32)],
        scratch_shapes=[
            pltpu.VMEM(packs[0].shape[1:], f32),
            pltpu.VMEM((2, length, width), bf16),
            ext,
            *(pltpu.VMEM((2,) + shape, dtype) for shape, dtype in scratch),
            pltpu.SemaphoreType.DMA((2, key_heads)),
            pltpu.SemaphoreType.DMA((2, results)),
        ],
        compiler_params=pltpu.CompilerParams(vmem_limit_bytes=44 << 20),
        name="local_stage",
    )(first, far(projected), near(halo), *(near(p) for p in packs))
    return *made, [(norm, p) for p in range(parts)]


def reading_kernel(number, index, first_ref, x_ref, halo_ref, pack_ref, *refs):
    written_ref, joint_ref, key_ref, norm_ref, out_ref, reach_ref, ext = refs
    heads = pl.num_programs(0) * V_GROUP
    g = pl.program_id(0)
    units = heads * number
    row, col = square_iotas()
    inside = row >= col
    gates = [
        pack_ref[index, pl.ds(c * heads + g * V_GROUP, V_GROUP)] for c in range(number)
    ]
    cumulative = running_sum(jnp.concatenate(gates, axis=0))
    bits = cumulative * LOG2E
    columns = jnp.transpose(bits, (1, 0))
    ext[0:HALO] = halo_ref[...].astype(f32)
    ext[HALO:] = x_ref[...].astype(f32)
    taps = pack_ref[index, pl.ds(2 * units + g * SEGMENTS * KW, KW)]
    for c in range(number):
        rows = slice(c * STRETCH, (c + 1) * STRETCH)
        query = convolved(ext, slice(0, DK), taps, c)
        gram = lax.dot_general(
            query, key_ref[0, rows], (((1,), (1,)), ((), ())), preferred_element_type=f32
        )
        log_row = norm_ref[0, pl.ds(g, 1), c]
        for j in range(V_GROUP):
            unit = c * V_GROUP + j
            sum_here = columns[:, unit : unit + 1]
            spread = sum_here - (bits[unit : unit + 1] - log_row)
            decay = jnp.exp2(jnp.where(inside, spread, -1e30))
            result = product((gram * decay).astype(bf16), written_ref[0, c, j])
            grown = jnp.exp2(sum_here)
            if c == 0:
                reached = result[:, DK:] + grown * query.astype(f32)
            else:
                result = result + grown * product(query, joint_ref[0, c, j])
                reached = result[:, DK:]
            out_ref[j, rows] = result[:, :DK].astype(bf16)
            reach_ref[j, rows] = reached.astype(bf16)


def reading_stage(first, step, parts, projected, halo, packs, index, kept):
    length, channels = projected.shape
    number = length // STRETCH
    key_heads = channels // parts // GROUP_CHANNELS
    heads = key_heads * V_GROUP
    written, joints, keys, norms = kept
    norm, norm_at = norms[step]
    query = lambda g, first: (0, (part_at(first[0], step, parts) * key_heads + g) * SEGMENTS)
    per_unit = pl.BlockSpec(
        (1, number, V_GROUP, STRETCH, 2 * DK), lambda g, first: (step, 0, g, 0, 0)
    )
    per_head = pl.BlockSpec((V_GROUP, length, DK), lambda g, first: (g, 0, 0))
    return pl.pallas_call(
        functools.partial(reading_kernel, number, index),
        grid_spec=pltpu.PrefetchScalarGridSpec(
            num_scalar_prefetch=1,
            grid=(key_heads,),
            in_specs=[
                pl.BlockSpec((length, DK), query),
                pl.BlockSpec((HALO, DK), query),
                pl.BlockSpec(packs.shape, lambda g, first: (0, 0, 0)),
                per_unit,
                per_unit,
                pl.BlockSpec((1, length, DK), lambda g, first: (step, 0, g)),
                pl.BlockSpec((1,) + norm.shape[1:], lambda g, first: (norm_at, 0, 0, 0)),
            ],
            out_specs=[per_head, per_head],
            scratch_shapes=[pltpu.VMEM((HALO + length, DK), f32)],
        ),
        out_shape=[pltpu.HBM((heads, length, DK), bf16)] * 2,
        compiler_params=pltpu.CompilerParams(vmem_limit_bytes=12 << 20),
        name="reading_stage",
    )(first, far(projected), halo, packs, far(written), far(joints), far(keys), norm)


def advance(joint, loss, gain):
    high = joint.astype(bf16)
    low = (joint - high.astype(f32)).astype(bf16)
    return joint + (product(loss, high) + product(loss, low)) + gain


def chain_kernel(run, summary_ref, state_ref, loss_ref, sub_ref, total_ref):
    devices, heads = summary_ref.shape[0], summary_ref.shape[1]
    row, col = square_iotas()
    eye = jnp.where(row == col, 1.0, 0.0).astype(f32)
    nothing = jnp.zeros((DK, DK), f32)
    start = jnp.concatenate([nothing, eye], axis=1)
    for h in range(heads):
        joint = [start] * (devices // run)
        for k in range(run):
            for i in range(devices // run):
                d = i * run + k
                state_ref[d, h] = joint[i][:, :DK]
                loss_ref[d, h] = (joint[i][:, DK:] - eye).astype(bf16)
                gain = jnp.concatenate([summary_ref[d, h, :, :DK].astype(f32), nothing], axis=1)
                joint[i] = advance(joint[i], summary_ref[d, h, :, DK:], gain)
        total = joint[0]
        for i in range(devices // run):
            sub_ref[i, h] = joint[i]
            if i > 0:
                gain = jnp.concatenate([joint[i][:, :DK], nothing], axis=1)
                total = advance(total, (joint[i][:, DK:] - eye).astype(bf16), gain)
        total_ref[h] = total


def chain_stage(summary):
    devices, heads = summary.shape[:2]
    run = 4 if devices % 4 == 0 else devices
    return pl.pallas_call(
        functools.partial(chain_kernel, run),
        in_specs=[VMEM],
        out_specs=[VMEM] * 4,
        out_shape=[
            pltpu.VMEM((devices, heads, DK, DK), f32),
            pltpu.VMEM((devices, heads, DK, DK), bf16),
            pltpu.VMEM((devices // run, heads, DK, 2 * DK), f32),
            pltpu.VMEM((heads, DK, 2 * DK), f32),
        ],
        compiler_params=pltpu.CompilerParams(vmem_limit_bytes=12 << 20),
        name="chain_stage",
    )(near(summary))


def entry_kernel(state_ref, loss_ref, sub_ref, entering_ref, start_ref):
    devices, heads = state_ref.shape[0], state_ref.shape[1]
    runs = sub_ref.shape[0]
    run = devices // runs
    row, col = square_iotas()
    eye = jnp.where(row == col, 1.0, 0.0).astype(f32)
    for h in range(heads):
        entering = [entering_ref[h]]
        for i in range(runs - 1):
            loss = (sub_ref[i, h, :, DK:] - eye).astype(bf16)
            entering.append(advance(entering[i], loss, sub_ref[i, h, :, :DK]))
        for d in range(devices):
            start = advance(entering[d // run], loss_ref[d, h], state_ref[d, h])
            start_ref[d, h] = start.astype(bf16)


def entry_stage(states, losses, subs, entering):
    devices, heads = states.shape[:2]
    return pl.pallas_call(
        entry_kernel,
        in_specs=[VMEM] * 4,
        out_specs=VMEM,
        out_shape=jax.ShapeDtypeStruct((devices, heads, DK, DK), bf16),
        compiler_params=pltpu.CompilerParams(vmem_limit_bytes=12 << 20),
        name="entry_stage",
    )(states, losses, subs, near(entering))


def finish_kernel(batch, first_ref, start_ref, gain_ref, *refs):
    reads, refs = refs[:-7], refs[-7:]
    out_ref, gain, held_local, held_reach, done, in_sems, out_sems = refs
    parts = len(reads) // 2
    heads = reads[0].shape[0]
    arriving, leaving = [], []
    gain_copy = pltpu.make_async_copy(gain_ref, gain, in_sems.at[0, out_sems.shape[0]])
    gain_copy.start()
    for p in range(parts):
        for b in range(heads // batch):
            at = pl.ds(b * batch, batch)
            into = pl.ds(p * heads + b * batch, batch)
            n = len(arriving)
            arriving.append(
                (
                    pltpu.make_async_copy(
                        reads[2 * p].at[at], held_local.at[into], in_sems.at[0, n]
                    ),
                    pltpu.make_async_copy(
                        reads[2 * p + 1].at[at], held_reach.at[into], in_sems.at[1, n]
                    ),
                )
            )
            for copy in arriving[-1]:
                copy.start()
    gain_copy.wait()
    for p in range(parts):
        part = part_at(first_ref[0], p, parts)
        for b in range(heads // batch):
            n = len(leaving)
            for copy in arriving[n]:
                copy.wait()
            for k in range(batch):
                h = p * heads + b * batch + k
                start = start_ref[part * heads + b * batch + k]
                result = held_local[h].astype(f32) + product(held_reach[h], start)
                mean = jnp.mean(result * result, axis=1, keepdims=True)
                scaled = result * lax.rsqrt(mean + 1e-06) * gain[...]
                done[:, h * DK : (h + 1) * DK] = scaled.astype(bf16)
            width = batch * DK
            to = pl.ds(pl.multiple_of((part * heads + b * batch) * DK, DK), width)
            leaving.append(
                pltpu.make_async_copy(
                    done.at[:, pl.ds(n * width, width)], out_ref.at[:, to], out_sems.at[n]
                )
            )
            leaving[-1].start()
    for copy in leaving:
        copy.wait()


def finish_stage(first, reads, starts, gain):
    heads, length, _ = reads[0][0].shape
    all_heads = starts.shape[0]
    batch = 2
    return pl.pallas_call(
        functools.partial(finish_kernel, batch),
        in_specs=[SMEM, VMEM, FAR] + [FAR] * (2 * len(reads)),
        out_specs=FAR,
        out_shape=pltpu.HBM((length, all_heads * DK), bf16),
        scratch_shapes=[
            pltpu.VMEM((1, DK), f32),
            pltpu.VMEM((all_heads, length, DK), bf16),
            pltpu.VMEM((all_heads, length, DK), bf16),
            pltpu.VMEM((length, all_heads * DK), bf16),
            pltpu.SemaphoreType.DMA((2, all_heads // batch + 1)),
            pltpu.SemaphoreType.DMA((all_heads // batch,)),
        ],
        compiler_params=pltpu.CompilerParams(vmem_limit_bytes=16 << 20),
        name="finish_stage",
    )(first, near(starts), far(gain.reshape(1, DK)), *(far(a) for read in reads for a in read))


def entering_state(total):
    outer = lax.axis_size("outer")
    if outer == 1:
        return jnp.zeros_like(total[..., :DK])
    if outer == 2:
        return lax.ppermute(total[..., :DK], "outer", [(0, 1)])
    everyone = lax.all_gather(total, "outer", axis=0)
    mine = lax.axis_index("outer")

    def step(i, state):
        piece = lax.dynamic_index_in_dim(everyone, i, 0, keepdims=False)
        moved = piece[..., :DK] + jnp.einsum(
            "hij,hjk->hik", piece[..., DK:], state, precision=lax.Precision.HIGHEST
        )
        return jnp.where(i < mine, moved, state)

    return lax.fori_loop(0, outer - 1, step, jnp.zeros_like(total[..., :DK]))


def per_device(projected, conv_weight, log_gate, write_rate, norm_gain):
    devices = lax.axis_size(ALL)
    parts = lax.axis_size("head")
    route = [(i, i + 1) for i in range(devices - 1)]
    arguments = (projected, log_gate, write_rate, conv_weight)
    if parts == 2:
        first = lax.axis_index("head").astype(jnp.int32).reshape(1)
        tail, mine, theirs = pack_stage(first, (1, 1), parts, *arguments)
        halo = lax.ppermute(tail, ALL, route)
        packs = [mine, lax.ppermute(theirs, "head", [(0, 1), (1, 0)])]
    else:
        first = jnp.zeros((1,), jnp.int32)
        tail, mine = pack_stage(first, (parts,), parts, *arguments)
        halo = lax.ppermute(tail, ALL, route)
        packs = [lax.all_to_all(mine, "head", 0, 0, tiled=True)]
    entries = [(pack, i) for pack in packs for i in range(pack.shape[0])]

    summary, *kept = local_stage(first, parts, projected, halo, packs)
    heads = summary.shape[0]
    members = lax.axis_size(NEAR)
    own = heads // members
    summary = lax.all_to_all(summary, NEAR, 0, 0, tiled=True)
    early = max(1, parts // 2)

    def reading(step):
        return reading_stage(first, step, parts, projected, halo, *entries[step], kept)

    reads = [reading(step) for step in range(early)]
    summary, reads = lax.optimization_barrier((summary, reads))
    *prefix, total = chain_stage(summary.reshape(members, own, DK, 2 * DK))
    starts = entry_stage(*prefix, entering_state(total))
    starts = lax.all_to_all(starts.reshape(heads, DK, DK), NEAR, 0, 0, tiled=True)
    reads += [reading(step) for step in range(early, parts)]
    return finish_stage(first, reads, starts, norm_gain)


def solution(mesh):
    seq, head = mesh.shape["seq"], mesh.shape["head"]
    inner = max(1, 16 // head)
    while seq % inner:
        inner //= 2
    layered = Mesh(mesh.devices.reshape(seq // inner, inner, head), ALL)
    in_specs = (
        P(ALL, None),
        P(None, "head"),
        P("head", ("outer", "inner")),
        P("head", ("outer", "inner")),
        P(),
    )
    return jax.shard_map(
        per_device, mesh=layered, in_specs=in_specs, out_specs=P(ALL, None), check_vma=False
    )
```

```python
import functools

import jax
import jax.numpy as jnp
from jax import lax
from jax.experimental import pallas as pl
from jax.experimental.pallas import tpu as pltpu
from jax.sharding import Mesh
from jax.sharding import PartitionSpec as P

DK = 128
V_GROUP = 2
KW = 4
STRETCH = 128
HALO = 8
BASE = 16
SEGMENTS = 2 + V_GROUP
GROUP_CHANNELS = (2 + V_GROUP) * DK
ALL = ("outer", "inner", "head")
NEAR = ("inner", "head")

f32 = jnp.float32
bf16 = jnp.bfloat16


LOG2E = 1.4426950408889634
VMEM = pl.BlockSpec(memory_space=pltpu.VMEM)
SMEM = pl.BlockSpec(memory_space=pltpu.SMEM)
FAR = pl.BlockSpec(memory_space=pltpu.HBM)


def near(array):
    return pltpu.with_memory_space_constraint(array, pltpu.VMEM)


def far(array):
    return pltpu.with_memory_space_constraint(array, pltpu.HBM)


def product(left, right):
    return jnp.dot(left, right, preferred_element_type=f32)


def part_at(first, step, parts):
    return lax.rem(first + step, parts)


def lanes_of(start):
    return pl.ds(pl.multiple_of(start, DK), DK)


def halves(array):
    high = array.astype(bf16)
    return high, (array - high.astype(f32)).astype(bf16)


def product_left(left, right):
    high, low = halves(left)
    both = product(jnp.concatenate([high, low], axis=0), right)
    return both[: left.shape[0]] + both[left.shape[0] :]


def convolved(ext, cols, taps, c):
    start = c * STRETCH + HALO - (KW - 1)
    total = ext[start : start + STRETCH, cols] * taps[0:1]
    for j in range(1, KW):
        total = total + ext[start + j : start + j + STRETCH, cols] * taps[j : j + 1]
    half = 0.5 * total
    return (half + half * jnp.tanh(half)).astype(bf16)


def running_sum(gates):
    lane = lax.broadcasted_iota(jnp.int32, gates.shape, 1)
    total = gates
    for k in (1, 2, 4, 8, 16, 32, 64):
        total = total + jnp.where(lane >= k, pltpu.roll(total, k, 1), 0.0)
    return total


def square_iotas():
    row = lax.broadcasted_iota(jnp.int32, (STRETCH, STRETCH), 0)
    col = lax.broadcasted_iota(jnp.int32, (STRETCH, STRETCH), 1)
    return row, col


def block_inverses(lower):
    units = len(lower)
    blocks = STRETCH // BASE
    small_lane = lax.broadcasted_iota(jnp.int32, (BASE, STRETCH), 1)
    small_row = lax.broadcasted_iota(jnp.int32, (BASE, STRETCH), 0)
    owner = small_lane // BASE
    packed = []
    for unit in range(units):
        piece = lower[unit][0:BASE]
        for b in range(1, blocks):
            piece = jnp.where(owner == b, lower[unit][b * BASE : (b + 1) * BASE], piece)
        packed.append(piece)
    half = BASE // 2
    upper = jnp.concatenate([piece[:half] for piece in packed], axis=0)
    under = jnp.concatenate([piece[half:] for piece in packed], axis=0)
    group_start = (lax.broadcasted_iota(jnp.int32, upper.shape, 1) // BASE) * BASE
    start = jnp.where(small_lane % BASE == small_row, 1.0, 0.0).astype(f32)
    shape = (units, half, STRETCH)
    top = jnp.broadcast_to(start[None, :half], shape)
    bottom = jnp.broadcast_to(start[None, half:], shape)
    for j in range(BASE - 1):
        pivot = top[:, j : j + 1, :] if j < half else bottom[:, j - half : j - half + 1, :]
        if j < half - 1:
            top = top - jnp.take_along_axis(upper, group_start + j, axis=1).reshape(shape) * pivot
        bottom = bottom - jnp.take_along_axis(under, group_start + j, axis=1).reshape(shape) * pivot
    solved = [jnp.concatenate([top[unit], bottom[unit]], axis=0) for unit in range(units)]

    rows = [
        [jnp.where(owner == b, solved[unit], 0.0) for b in range(blocks)] for unit in range(units)
    ]
    size = BASE
    while size < STRETCH:
        per = size // BASE
        odd = [b for b in range(blocks) if (b // per) % 2 == 1]
        firsts = []
        for unit in range(units):
            crossing = [
                jnp.where(
                    small_lane // size == (b // per) - 1,
                    lower[unit][b * BASE : (b + 1) * BASE],
                    0.0,
                )
                for b in odd
            ]
            firsts.append(
                product(
                    jnp.concatenate(crossing, axis=0).astype(bf16),
                    jnp.concatenate(rows[unit], axis=0).astype(bf16),
                ).astype(bf16)
            )
        for unit in range(units):
            laid = [jnp.zeros((BASE, STRETCH), bf16)] * blocks
            for i, b in enumerate(odd):
                laid[b] = firsts[unit][i * BASE : (i + 1) * BASE]
            odd_rows = jnp.concatenate([rows[unit][b] for b in odd], axis=0)
            updated = odd_rows - product(odd_rows.astype(bf16), jnp.concatenate(laid, axis=0))
            for i, b in enumerate(odd):
                rows[unit][b] = updated[i * BASE : (i + 1) * BASE]
        size *= 2
    return [jnp.concatenate(rows[unit], axis=0) for unit in range(units)]


def pack_kernel(parts, first_ref, x_ref, gate_ref, rate_ref, taps_ref, halo_ref, *pack_refs):
    heads = gate_ref.shape[0]
    length = gate_ref.shape[1] // parts
    number = length // STRETCH
    segments = taps_ref.shape[1] // DK
    halo_ref[...] = x_ref[...]
    base = 2 * number * heads
    slots = [(ref, i) for ref in pack_refs for i in range(ref.shape[0])]
    for step, (ref, i) in enumerate(slots):
        first = part_at(first_ref[0], step, parts) * length
        for c in range(number):
            lanes = lanes_of(first + c * STRETCH)
            ref[i, c * heads : (c + 1) * heads] = gate_ref[:, lanes]
            ref[i, (number + c) * heads : (number + c + 1) * heads] = rate_ref[:, lanes]
        for segment in range(segments):
            rows = slice(base + segment * KW, base + (segment + 1) * KW)
            ref[i, rows] = taps_ref[:, segment * DK : (segment + 1) * DK].astype(f32)


def pack_stage(first, stacks, parts, projected, log_gate, write_rate, conv_weight):
    length, channels = projected.shape
    heads = log_gate.shape[0]
    rows = 2 * (length // STRETCH) * heads + conv_weight.shape[1] // DK * KW
    whole = lambda array: pl.BlockSpec(array.shape, lambda i: (0, 0))
    return pl.pallas_call(
        functools.partial(pack_kernel, parts),
        grid=(1,),
        in_specs=[
            SMEM,
            pl.BlockSpec((HALO, channels), lambda i: (length // HALO - 1, 0)),
            whole(log_gate),
            whole(write_rate),
            whole(conv_weight),
        ],
        out_specs=[VMEM] * (1 + len(stacks)),
        out_shape=[pltpu.VMEM((HALO, channels), bf16)]
        + [pltpu.VMEM((count, rows, DK), f32) for count in stacks],
        compiler_params=pltpu.CompilerParams(vmem_limit_bytes=2 << 20),
        name="pack_stage",
    )(first, far(projected), far(log_gate), far(write_rate), far(conv_weight))


def local_body(number, part, halo_ref, pack, block, ext, kept, norm_ref, arrived, ready):
    key_ref, summary_ref, written_ref, joint_ref = kept
    key_heads = norm_ref.shape[1]
    width = key_heads * GROUP_CHANNELS
    heads = key_heads * V_GROUP
    units = heads * number
    row, col = square_iotas()
    below = row > col
    eye = jnp.where(row == col, 1.0, 0.0).astype(f32)

    rates = pack[units : 2 * units]
    cumulative = running_sum(pack[0:units])
    grown = jnp.exp(cumulative)
    tail = jnp.exp(cumulative[:, STRETCH - 1 : STRETCH] - cumulative)
    bits = cumulative * LOG2E
    columns = jnp.transpose(bits + jnp.log2(rates), (1, 0))
    where = [(c, g) for g in range(key_heads) for c in range(number)]

    def units_of(c, g):
        return [(j, c * heads + g * V_GROUP + j) for j in range(V_GROUP)]

    def channels(c, g, kind):
        segment = g * SEGMENTS + kind
        cols = slice(segment * DK, (segment + 1) * DK)
        if c == 0:
            ext[0:HALO, cols] = halo_ref[:, lanes_of(part * width + segment * DK)].astype(f32)
            ext[HALO:, cols] = block[:, cols].astype(f32)
        at = 2 * units + segment * KW
        return convolved(ext, cols, pack[at : at + KW], c)

    keys, inverses, lower = {}, {}, [None] * units
    for c, g in where:
        if c == 0:
            arrived(g)
        k = channels(c, g, 1)
        keys[c, g] = k
        key_ref[c * STRETCH : (c + 1) * STRETCH, g * DK : (g + 1) * DK] = k
        gram = lax.dot_general(k, k, (((1,), (1,)), ((), ())), preferred_element_type=f32)
        diagonal = gram * eye
        sum_row = jnp.sum(diagonal, axis=0, keepdims=True) + 1e-06
        sum_col = jnp.sum(diagonal, axis=1, keepdims=True) + 1e-06
        inverses[c, g] = lax.rsqrt(sum_row)
        log_row, log_col = -0.5 * jnp.log2(sum_row), -0.5 * jnp.log2(sum_col)
        norm_ref[0, g, c : c + 1] = log_row
        for j, unit in units_of(c, g):
            spread = (columns[:, unit : unit + 1] + log_col) - (bits[unit : unit + 1] - log_row)
            lower[unit] = gram * jnp.exp2(jnp.where(below, spread, -1e30))

    ready(0)
    solved = block_inverses(lower)

    fresh, carried, scaled = [None] * units, [None] * units, [None] * units
    for c, g in where:
        turned = jnp.transpose(keys[c, g].astype(f32), (1, 0)) * inverses[c, g]
        for j, unit in units_of(c, g):
            at = slice(unit, unit + 1)
            by_rate = solved[unit] * rates[at]
            fresh[unit] = product_left(by_rate, channels(c, g, 2 + j))
            by_rate = by_rate * (grown[at] * inverses[c, g])
            carried[unit] = product_left(by_rate, keys[c, g])
            scaled[unit] = (turned * tail[at]).astype(bf16)

    nothing = jnp.zeros((STRETCH, DK), f32)
    joint = [jnp.concatenate([jnp.zeros((DK, DK), f32), eye], axis=1)] * heads
    for c in range(number):
        for head in range(heads):
            unit = c * heads + head
            if c == 0:
                written = jnp.concatenate([fresh[unit], -carried[unit]], axis=1)
            else:
                start = joint[head].astype(bf16)
                joint_ref[c - 1, head] = start
                written = jnp.concatenate([fresh[unit], nothing], axis=1) - product(
                    carried[unit].astype(bf16), start
                )
            written = written.astype(bf16)
            written_ref[c, head] = written
            decay = grown[unit : unit + 1, STRETCH - 1 : STRETCH]
            joint[head] = joint[head] * decay + product(scaled[unit], written)
        ready(2 + c)
        if c > 0:
            ready(1 + number + c)
    for head in range(heads):
        summary_ref[head, :, :DK] = joint[head][:, :DK].astype(bf16)
        summary_ref[head, :, DK:] = (joint[head][:, DK:] - eye).astype(bf16)
    ready(1)


def channel_copies(base, key_heads, x_ref, block, sems):
    used = (SEGMENTS - 1) * DK
    copies = []
    for g in range(key_heads):
        source = pl.ds(pl.multiple_of(base + (g * SEGMENTS + 1) * DK, DK), used)
        target = pl.ds((g * SEGMENTS + 1) * DK, used)
        copies.append(
            pltpu.make_async_copy(x_ref.at[:, source], block.at[:, target], sems.at[g])
        )
    return copies


def kept_copies(number, step, place, kept, outs, sems):
    key_ref, summary_ref, written_ref, joint_ref = kept
    pairs = [(key_ref, outs[3].at[step]), (summary_ref, outs[0].at[place])]
    pairs += [(written_ref.at[c], outs[1].at[step, c]) for c in range(number)]
    pairs += [(joint_ref.at[c - 1], outs[2].at[step, c]) for c in range(1, number)]
    return [
        pltpu.make_async_copy(source, target, sems.at[i]) for i, (source, target) in enumerate(pairs)
    ]


def first_kernel(number, parts, first_ref, x_ref, halo_ref, pack_ref, *refs):
    kept, (norm_ref, other, block, ext, sems, other_sems) = refs[:4], refs[4:]
    key_heads = norm_ref.shape[1]
    width = key_heads * GROUP_CHANNELS
    part, next_part = part_at(first_ref[0], 0, parts), part_at(first_ref[0], 1, parts)
    coming = channel_copies(part * width, key_heads, x_ref, block, sems)
    others = channel_copies(next_part * width, key_heads, x_ref, other, other_sems)
    for copy in coming + others:
        copy.start()
    local_body(
        number,
        part,
        halo_ref,
        pack_ref.at[0],
        block,
        ext,
        kept,
        norm_ref,
        lambda g: coming[g].wait(),
        lambda i: None,
    )
    for copy in others:
        copy.wait()


def second_kernel(number, parts, first_ref, halo_ref, pack_ref, block, *refs):
    before, outs, norm_ref, (ext, *kept, before_sems, sems) = refs[:4], refs[4:8], refs[8], refs[9:]
    heads = norm_ref.shape[1] * V_GROUP
    old, part = part_at(first_ref[0], 0, parts), part_at(first_ref[0], 1, parts)
    leaving = kept_copies(number, 0, pl.ds(old * heads, heads), before, outs, before_sems)
    for copy in leaving:
        copy.start()
    going = kept_copies(number, 1, pl.ds(part * heads, heads), kept, outs, sems)
    local_body(
        number,
        part,
        halo_ref,
        pack_ref.at[0],
        block,
        ext,
        kept,
        norm_ref,
        lambda g: None,
        lambda i: going[i].start(),
    )
    for copy in leaving + going:
        copy.wait()


def local_kernel(number, parts, stacks, first_ref, x_ref, halo_ref, *refs):
    pack_refs, refs = refs[: len(stacks)], refs[len(stacks) :]
    outs, norm_ref = refs[:4], refs[4]
    pack, blocks, ext, *held, in_sems, out_sems = refs[5:]
    step = pl.program_id(0)
    key_heads = norm_ref.shape[1]
    width = key_heads * GROUP_CHANNELS
    heads = key_heads * V_GROUP

    def arriving(at):
        here = lax.rem(at, 2)
        base = part_at(first_ref[0], at, parts) * width
        return channel_copies(base, key_heads, x_ref, blocks.at[here], in_sems.at[here])

    def leaving(at):
        here = lax.rem(at, 2)
        place = pl.ds(part_at(first_ref[0], at, parts) * heads, heads)
        kept = [ref.at[here] for ref in held]
        return kept_copies(number, at, place, kept, outs, out_sems.at[here])

    @pl.when(step == 0)
    def _():
        for copy in arriving(step):
            copy.start()

    @pl.when(step + 1 < pl.num_programs(0))
    def _():
        for copy in arriving(step + 1):
            copy.start()

    coming, going = arriving(step), leaving(step)
    entries = [(ref, i) for ref in pack_refs for i in range(ref.shape[0])]
    for n, (ref, i) in enumerate(entries):

        @pl.when(step == n)
        def _():
            pack[...] = ref[i]

    slot = lax.rem(step, 2)
    local_body(
        number,
        part_at(first_ref[0], step, parts),
        halo_ref,
        pack,
        blocks.at[slot],
        ext,
        [ref.at[slot] for ref in held],
        norm_ref,
        lambda g: coming[g].wait(),
        lambda i: going[i].start(),
    )

    @pl.when(step > 0)
    def _():
        for copy in leaving(step - 1):
            copy.wait()

    @pl.when(step + 1 == pl.num_programs(0))
    def _():
        for copy in going:
            copy.wait()


def kept_scratch(number, heads, length):
    return [
        ((length, heads // V_GROUP * DK), bf16),
        ((heads, DK, 2 * DK), bf16),
        ((number, heads, STRETCH, 2 * DK), bf16),
        ((max(1, number - 1), heads, STRETCH, 2 * DK), bf16),
    ]


def kept_arrays(parts, number, heads, length):
    per_unit = (parts, number, heads, STRETCH, 2 * DK)
    return [
        pltpu.HBM((heads * parts, DK, 2 * DK), bf16),
        pltpu.HBM(per_unit, bf16),
        pltpu.HBM(per_unit, bf16),
        pltpu.HBM((parts, length, heads // V_GROUP * DK), bf16),
    ]


def local_stage(first, parts, projected, halo, packs):
    length, channels = projected.shape
    number = length // STRETCH
    width = channels // parts
    key_heads = width // GROUP_CHANNELS
    heads = key_heads * V_GROUP
    scratch = kept_scratch(number, heads, length)
    kept = kept_arrays(parts, number, heads, length)
    norms = (1, key_heads, number, STRETCH)
    ext = pltpu.VMEM((HALO + length, width), f32)
    results = 2 * number + 1
    if len(packs) == 2:
        *before, norm, block = pl.pallas_call(
            functools.partial(first_kernel, number, parts),
            in_specs=[SMEM, FAR, VMEM, VMEM],
            out_specs=[VMEM] * 6,
            out_shape=[pltpu.VMEM(*shape) for shape in scratch]
            + [pltpu.VMEM(norms, f32), pltpu.VMEM((length, width), bf16)],
            scratch_shapes=[
                pltpu.VMEM((length, width), bf16),
                ext,
                pltpu.SemaphoreType.DMA((key_heads,)),
                pltpu.SemaphoreType.DMA((key_heads,)),
            ],
            compiler_params=pltpu.CompilerParams(vmem_limit_bytes=24 << 20),
            name="first_stage",
        )(first, far(projected), near(halo), near(packs[0]))
        *made, other_norm = pl.pallas_call(
            functools.partial(second_kernel, number, parts),
            in_specs=[SMEM] + [VMEM] * 7,
            out_specs=[FAR] * 4 + [VMEM],
            out_shape=kept + [pltpu.VMEM(norms, f32)],
            scratch_shapes=[ext]
            + [pltpu.VMEM(*shape) for shape in scratch]
            + [pltpu.SemaphoreType.DMA((results,))] * 2,
            compiler_params=pltpu.CompilerParams(vmem_limit_bytes=24 << 20),
            name="second_stage",
        )(first, near(halo), near(packs[1]), block, *before)
        return *made, [(norm, 0), (other_norm, 0)]
    *made, norm = pl.pallas_call(
        functools.partial(local_kernel, number, parts, tuple(p.shape[0] for p in packs)),
        grid=(parts,),
        in_specs=[SMEM, FAR] + [VMEM] * (1 + len(packs)),
        out_specs=[FAR] * 4 + [pl.BlockSpec(norms, lambda p: (p, 0, 0, 0))],
        out_shape=kept + [jax.ShapeDtypeStruct((parts,) + norms[1:], f32)],
        scratch_shapes=[
            pltpu.VMEM(packs[0].shape[1:], f32),
            pltpu.VMEM((2, length, width), bf16),
            ext,
            *(pltpu.VMEM((2,) + shape, dtype) for shape, dtype in scratch),
            pltpu.SemaphoreType.DMA((2, key_heads)),
            pltpu.SemaphoreType.DMA((2, results)),
        ],
        compiler_params=pltpu.CompilerParams(vmem_limit_bytes=44 << 20),
        name="local_stage",
    )(first, far(projected), near(halo), *(near(p) for p in packs))
    return *made, [(norm, p) for p in range(parts)]


def reading_kernel(number, index, first_ref, x_ref, halo_ref, pack_ref, *refs):
    written_ref, joint_ref, key_ref, norm_ref, out_ref, reach_ref, ext = refs
    heads = pl.num_programs(0) * V_GROUP
    g = pl.program_id(0)
    units = heads * number
    row, col = square_iotas()
    inside = row >= col
    gates = [
        pack_ref[index, pl.ds(c * heads + g * V_GROUP, V_GROUP)] for c in range(number)
    ]
    cumulative = running_sum(jnp.concatenate(gates, axis=0))
    bits = cumulative * LOG2E
    columns = jnp.transpose(bits, (1, 0))
    ext[0:HALO] = halo_ref[...].astype(f32)
    ext[HALO:] = x_ref[...].astype(f32)
    taps = pack_ref[index, pl.ds(2 * units + g * SEGMENTS * KW, KW)]
    for c in range(number):
        rows = slice(c * STRETCH, (c + 1) * STRETCH)
        query = convolved(ext, slice(0, DK), taps, c)
        gram = lax.dot_general(
            query, key_ref[0, rows], (((1,), (1,)), ((), ())), preferred_element_type=f32
        )
        log_row = norm_ref[0, pl.ds(g, 1), c]
        for j in range(V_GROUP):
            unit = c * V_GROUP + j
            sum_here = columns[:, unit : unit + 1]
            spread = sum_here - (bits[unit : unit + 1] - log_row)
            decay = jnp.exp2(jnp.where(inside, spread, -1e30))
            result = product((gram * decay).astype(bf16), written_ref[0, c, j])
            grown = jnp.exp2(sum_here)
            if c == 0:
                reached = result[:, DK:] + grown * query.astype(f32)
            else:
                result = result + grown * product(query, joint_ref[0, c, j])
                reached = result[:, DK:]
            out_ref[j, rows] = result[:, :DK].astype(bf16)
            reach_ref[j, rows] = reached.astype(bf16)


def reading_stage(first, step, parts, projected, halo, packs, index, kept):
    length, channels = projected.shape
    number = length // STRETCH
    key_heads = channels // parts // GROUP_CHANNELS
    heads = key_heads * V_GROUP
    written, joints, keys, norms = kept
    norm, norm_at = norms[step]
    query = lambda g, first: (0, (part_at(first[0], step, parts) * key_heads + g) * SEGMENTS)
    per_unit = pl.BlockSpec(
        (1, number, V_GROUP, STRETCH, 2 * DK), lambda g, first: (step, 0, g, 0, 0)
    )
    per_head = pl.BlockSpec((V_GROUP, length, DK), lambda g, first: (g, 0, 0))
    return pl.pallas_call(
        functools.partial(reading_kernel, number, index),
        grid_spec=pltpu.PrefetchScalarGridSpec(
            num_scalar_prefetch=1,
            grid=(key_heads,),
            in_specs=[
                pl.BlockSpec((length, DK), query),
                pl.BlockSpec((HALO, DK), query),
                pl.BlockSpec(packs.shape, lambda g, first: (0, 0, 0)),
                per_unit,
                per_unit,
                pl.BlockSpec((1, length, DK), lambda g, first: (step, 0, g)),
                pl.BlockSpec((1,) + norm.shape[1:], lambda g, first: (norm_at, 0, 0, 0)),
            ],
            out_specs=[per_head, per_head],
            scratch_shapes=[pltpu.VMEM((HALO + length, DK), f32)],
        ),
        out_shape=[pltpu.HBM((heads, length, DK), bf16)] * 2,
        compiler_params=pltpu.CompilerParams(vmem_limit_bytes=12 << 20),
        name="reading_stage",
    )(first, far(projected), halo, packs, far(written), far(joints), far(keys), norm)


def advance(joint, loss, gain):
    high = joint.astype(bf16)
    low = (joint - high.astype(f32)).astype(bf16)
    return joint + (product(loss, high) + product(loss, low)) + gain


def chain_kernel(run, summary_ref, state_ref, loss_ref, sub_ref, total_ref):
    devices, heads = summary_ref.shape[0], summary_ref.shape[1]
    row, col = square_iotas()
    eye = jnp.where(row == col, 1.0, 0.0).astype(f32)
    nothing = jnp.zeros((DK, DK), f32)
    start = jnp.concatenate([nothing, eye], axis=1)
    for h in range(heads):
        joint = [start] * (devices // run)
        for k in range(run):
            for i in range(devices // run):
                d = i * run + k
                state_ref[d, h] = joint[i][:, :DK]
                loss_ref[d, h] = (joint[i][:, DK:] - eye).astype(bf16)
                gain = jnp.concatenate([summary_ref[d, h, :, :DK].astype(f32), nothing], axis=1)
                joint[i] = advance(joint[i], summary_ref[d, h, :, DK:], gain)
        total = joint[0]
        for i in range(devices // run):
            sub_ref[i, h] = joint[i]
            if i > 0:
                gain = jnp.concatenate([joint[i][:, :DK], nothing], axis=1)
                total = advance(total, (joint[i][:, DK:] - eye).astype(bf16), gain)
        total_ref[h] = total


def chain_stage(summary):
    devices, heads = summary.shape[:2]
    run = 4 if devices % 4 == 0 else devices
    return pl.pallas_call(
        functools.partial(chain_kernel, run),
        in_specs=[VMEM],
        out_specs=[VMEM] * 4,
        out_shape=[
            pltpu.VMEM((devices, heads, DK, DK), f32),
            pltpu.VMEM((devices, heads, DK, DK), bf16),
            pltpu.VMEM((devices // run, heads, DK, 2 * DK), f32),
            pltpu.VMEM((heads, DK, 2 * DK), f32),
        ],
        compiler_params=pltpu.CompilerParams(vmem_limit_bytes=12 << 20),
        name="chain_stage",
    )(near(summary))


def entry_kernel(state_ref, loss_ref, sub_ref, entering_ref, start_ref):
    devices, heads = state_ref.shape[0], state_ref.shape[1]
    runs = sub_ref.shape[0]
    run = devices // runs
    row, col = square_iotas()
    eye = jnp.where(row == col, 1.0, 0.0).astype(f32)
    for h in range(heads):
        entering = [entering_ref[h]]
        for i in range(runs - 1):
            loss = (sub_ref[i, h, :, DK:] - eye).astype(bf16)
            entering.append(advance(entering[i], loss, sub_ref[i, h, :, :DK]))
        for d in range(devices):
            start = advance(entering[d // run], loss_ref[d, h], state_ref[d, h])
            start_ref[d, h] = start.astype(bf16)


def entry_stage(states, losses, subs, entering):
    devices, heads = states.shape[:2]
    return pl.pallas_call(
        entry_kernel,
        in_specs=[VMEM] * 4,
        out_specs=VMEM,
        out_shape=jax.ShapeDtypeStruct((devices, heads, DK, DK), bf16),
        compiler_params=pltpu.CompilerParams(vmem_limit_bytes=12 << 20),
        name="entry_stage",
    )(states, losses, subs, near(entering))


def finish_kernel(batch, first_ref, start_ref, gain_ref, *refs):
    reads, refs = refs[:-7], refs[-7:]
    out_ref, gain, held_local, held_reach, done, in_sems, out_sems = refs
    parts = len(reads) // 2
    heads = reads[0].shape[0]
    arriving, leaving = [], []
    gain_copy = pltpu.make_async_copy(gain_ref, gain, in_sems.at[0, out_sems.shape[0]])
    gain_copy.start()
    for p in range(parts):
        for b in range(heads // batch):
            at = pl.ds(b * batch, batch)
            into = pl.ds(p * heads + b * batch, batch)
            n = len(arriving)
            arriving.append(
                (
                    pltpu.make_async_copy(
                        reads[2 * p].at[at], held_local.at[into], in_sems.at[0, n]
                    ),
                    pltpu.make_async_copy(
                        reads[2 * p + 1].at[at], held_reach.at[into], in_sems.at[1, n]
                    ),
                )
            )
            for copy in arriving[-1]:
                copy.start()
    gain_copy.wait()
    for p in range(parts):
        part = part_at(first_ref[0], p, parts)
        for b in range(heads // batch):
            n = len(leaving)
            for copy in arriving[n]:
                copy.wait()
            for k in range(batch):
                h = p * heads + b * batch + k
                start = start_ref[part * heads + b * batch + k]
                result = held_local[h].astype(f32) + product(held_reach[h], start)
                mean = jnp.mean(result * result, axis=1, keepdims=True)
                scaled = result * lax.rsqrt(mean + 1e-06) * gain[...]
                done[:, h * DK : (h + 1) * DK] = scaled.astype(bf16)
            width = batch * DK
            to = pl.ds(pl.multiple_of((part * heads + b * batch) * DK, DK), width)
            leaving.append(
                pltpu.make_async_copy(
                    done.at[:, pl.ds(n * width, width)], out_ref.at[:, to], out_sems.at[n]
                )
            )
            leaving[-1].start()
    for copy in leaving:
        copy.wait()


def finish_stage(first, reads, starts, gain):
    heads, length, _ = reads[0][0].shape
    all_heads = starts.shape[0]
    batch = min(4, heads)
    return pl.pallas_call(
        functools.partial(finish_kernel, batch),
        in_specs=[SMEM, VMEM, FAR] + [FAR] * (2 * len(reads)),
        out_specs=FAR,
        out_shape=pltpu.HBM((length, all_heads * DK), bf16),
        scratch_shapes=[
            pltpu.VMEM((1, DK), f32),
            pltpu.VMEM((all_heads, length, DK), bf16),
            pltpu.VMEM((all_heads, length, DK), bf16),
            pltpu.VMEM((length, all_heads * DK), bf16),
            pltpu.SemaphoreType.DMA((2, all_heads // batch + 1)),
            pltpu.SemaphoreType.DMA((all_heads // batch,)),
        ],
        compiler_params=pltpu.CompilerParams(vmem_limit_bytes=16 << 20),
        name="finish_stage",
    )(first, near(starts), far(gain.reshape(1, DK)), *(far(a) for read in reads for a in read))


def entering_state(total):
    outer = lax.axis_size("outer")
    if outer == 1:
        return jnp.zeros_like(total[..., :DK])
    if outer == 2:
        return lax.ppermute(total[..., :DK], "outer", [(0, 1)])
    everyone = lax.all_gather(total, "outer", axis=0)
    mine = lax.axis_index("outer")

    def step(i, state):
        piece = lax.dynamic_index_in_dim(everyone, i, 0, keepdims=False)
        moved = piece[..., :DK] + jnp.einsum(
            "hij,hjk->hik", piece[..., DK:], state, precision=lax.Precision.HIGHEST
        )
        return jnp.where(i < mine, moved, state)

    return lax.fori_loop(0, outer - 1, step, jnp.zeros_like(total[..., :DK]))


def per_device(projected, conv_weight, log_gate, write_rate, norm_gain):
    devices = lax.axis_size(ALL)
    parts = lax.axis_size("head")
    route = [(i, i + 1) for i in range(devices - 1)]
    arguments = (projected, log_gate, write_rate, conv_weight)
    if parts == 2:
        first = lax.axis_index("head").astype(jnp.int32).reshape(1)
        tail, mine, theirs = pack_stage(first, (1, 1), parts, *arguments)
        halo = lax.ppermute(tail, ALL, route)
        packs = [mine, lax.ppermute(theirs, "head", [(0, 1), (1, 0)])]
    else:
        first = jnp.zeros((1,), jnp.int32)
        tail, mine = pack_stage(first, (parts,), parts, *arguments)
        halo = lax.ppermute(tail, ALL, route)
        packs = [lax.all_to_all(mine, "head", 0, 0, tiled=True)]
    entries = [(pack, i) for pack in packs for i in range(pack.shape[0])]

    summary, *kept = local_stage(first, parts, projected, halo, packs)
    heads = summary.shape[0]
    members = lax.axis_size(NEAR)
    own = heads // members
    summary = lax.all_to_all(summary, NEAR, 0, 0, tiled=True)
    early = max(1, parts // 2)

    def reading(step):
        return reading_stage(first, step, parts, projected, halo, *entries[step], kept)

    reads = [reading(step) for step in range(early)]
    summary, reads = lax.optimization_barrier((summary, reads))
    *prefix, total = chain_stage(summary.reshape(members, own, DK, 2 * DK))
    starts = entry_stage(*prefix, entering_state(total))
    starts = lax.all_to_all(starts.reshape(heads, DK, DK), NEAR, 0, 0, tiled=True)
    reads += [reading(step) for step in range(early, parts)]
    return finish_stage(first, reads, starts, norm_gain)


def solution(mesh):
    seq, head = mesh.shape["seq"], mesh.shape["head"]
    inner = max(1, 16 // head)
    while seq % inner:
        inner //= 2
    layered = Mesh(mesh.devices.reshape(seq // inner, inner, head), ALL)
    in_specs = (
        P(ALL, None),
        P(None, "head"),
        P("head", ("outer", "inner")),
        P("head", ("outer", "inner")),
        P(),
    )
    return jax.shard_map(
        per_device, mesh=layered, in_specs=in_specs, out_specs=P(ALL, None), check_vma=False
    )
```
